32 devices in a mesh: lon: 16 (over z, x, core), lat: 2 (over y).
Axes of the slice: x: 2, y: 2, z: 4, core: 2. Of those that a mesh axis runs over, the one named last changes fastest.
Arguments:
- state: float32 [5, 1, 5760, 256], P(None, None, 'lon', 'lat'), may hold values from -3 to 3
- cutoffs: int32 [2, 128], replicated, may hold values from 1 to 2879, as said below
Outputs:
- advanced: float32 [5, 1, 5760, 256], P(None, None, 'lon', 'lat')
The draws below stay inside these ranges and needn't reach their ends.
Inputs may be any that keep to these rules, and one draw needn't show every extreme that they name: cutoffs[0, j] is the highest zonal wavenumber kept in row j and cutoffs[1, j] that of row 255 - j; in both caps the row at the pole keeps 1 and row 127 from the pole keeps 2880 - 1.
All inputs are finite; a program needn't handle non-finite values.
Results may differ from the reference program's by a relative error of at most 0.0003.
Values sent between devices are 32-bit elements; how exact they have to be, the bound alone decides.
A program may use at most 64 MiB of HBM per device.

```python
import jax
import jax.numpy as jnp
from jax import lax

NLON = 5760
NMODES = 2880
FIELDS = 5
SUBSTEPS = 2
LEV = 1
LAT_DEV = 128
NLAT = 256


def draw_state(key, part):
    rough_key = jax.random.fold_in(key, 11)
    wave_key = jax.random.fold_in(key, 23)
    full_shape = (FIELDS, LEV, NLON, NLAT)
    rough_part = jnp.clip(jax.random.normal(rough_key, full_shape, jnp.float32), -3.0, 3.0)
    longitudes = jnp.arange(NLON, dtype=jnp.int32)
    for wave_term in range(8):
        term_keys = jax.random.split(jax.random.fold_in(wave_key, wave_term), 3)
        number = jax.random.randint(term_keys[0], (), 1, NMODES, dtype=jnp.int32)
        amplitude = jnp.clip(0.25 * jax.random.normal(term_keys[1], (FIELDS, LEV, 1, NLAT), jnp.float32), -0.3, 0.3)
        offset = jax.random.uniform(term_keys[2], (FIELDS, LEV, 1, NLAT), jnp.float32, 0.0, 2.0 * jnp.pi)
        wave_phase = (longitudes * number % NLON).astype(jnp.float32) * (2.0 * jnp.pi / NLON)
        rough_part = rough_part + amplitude * jnp.cos(wave_phase[None, None, :, None] + offset)
    field_scale = jnp.array([0.2, 0.5, 0.5, 0.2, 0.5], dtype=jnp.float32)[:, None, None, None]
    centre = jnp.array([1.0, 0.0, 0.0, 1.0, 0.0], dtype=jnp.float32)[:, None, None, None]
    return centre + field_scale * rough_part


def draw_cutoffs(key, part):
    row_index = jnp.arange(LAT_DEV, dtype=jnp.int32)
    ceiling = 1 + (NMODES - 2) * row_index // (LAT_DEV - 1)
    lowered = jax.random.randint(key, (2, LAT_DEV), 0, 1 << 20, dtype=jnp.int32) % (ceiling // 4 + 1)[None, :]
    chosen = ceiling[None, :] - lowered
    chosen = chosen.at[:, 0].set(1).at[:, LAT_DEV - 1].set(NMODES - 1)
    return chosen.astype(jnp.int32)


def setup_inputs(seed: int = 0) -> dict:
    arg_keys = jax.random.split(jax.random.key(seed), 3)
    return {
        "state": draw_state(jax.random.fold_in(arg_keys[2], 71), 0),
        "cutoffs": draw_cutoffs(jax.random.fold_in(arg_keys[2], 71), 0),
    }


time_step = 0.5
gravity_scale = 0.25
coriolis_scale = 0.5
wind_sign = (1.0, -1.0, -1.0, 1.0, 1.0)


def interface_flux(halo_padded, transported_field, advection_axis, extent_length):
    def shifted(offset):
        return lax.slice_in_dim(halo_padded, offset, offset + extent_length + 1, axis=advection_axis)

    far_west, mid_west, near_west, centre, near_east, far_east = [shifted(offset) for offset in range(6)]
    interface_velocity = 0.5 * (lax.slice_in_dim(transported_field, 2, extent_length + 3, axis=advection_axis) + lax.slice_in_dim(transported_field, 3, extent_length + 4, axis=advection_axis))
    central = (37.0 * (centre + near_west) - 8.0 * (near_east + mid_west) + (far_east + far_west)) / 60.0
    upwind = ((far_east - far_west) - 5.0 * (near_east - mid_west) + 10.0 * (centre - near_west)) / 60.0
    return interface_velocity * central - jnp.abs(interface_velocity) * upwind


def latitude_rows(first_row, row_count, total_rows):
    centres = (first_row + jnp.arange(row_count, dtype=jnp.int32)).astype(jnp.float32) + 0.5
    centre_cos = jnp.sin(centres * (jnp.pi / total_rows))
    centre_sin = -jnp.cos(centres * (jnp.pi / total_rows))
    faces = first_row + jnp.arange(row_count + 1, dtype=jnp.int32)
    face_cos = jnp.sin(jnp.minimum(faces, total_rows - faces).astype(jnp.float32) * (jnp.pi / total_rows))
    return centre_cos, centre_sin, face_cos


def geopotential(fields):
    layer_mass = fields[0] * fields[3]
    return gravity_scale * jnp.flip(jnp.cumsum(jnp.flip(layer_mass, 0), axis=0), 0)


def truncate(zonal_rows, cutoff_row):
    spectrum = jnp.fft.rfft(zonal_rows, axis=1)
    wave_number = jnp.arange(spectrum.shape[1], dtype=jnp.int32)
    kept_modes = wave_number[:, None] <= cutoff_row[None, :]
    return jnp.fft.irfft(jnp.where(kept_modes, spectrum, 0.0), n=zonal_rows.shape[1], axis=1)


def level_update(lon_level, lat_level, fields, phi_lon, phi_lat, geometry, cutoffs):
    centre_cos, centre_sin, face_cos = geometry
    lon_total = fields.shape[1]
    lat_total = fields.shape[2]
    face_fluxes = interface_flux(lon_level, lon_level[1:2], 1, lon_total)
    zonal = face_fluxes[:, :-1] - face_fluxes[:, 1:]
    height_slope = 0.5 * (phi_lon[4:lon_total + 4] - phi_lon[2:lon_total + 2])
    zonal = jnp.concatenate([zonal[:1], zonal[1:2] - height_slope[None], zonal[2:]], axis=0)
    zonal = zonal / centre_cos
    band_rows = cutoffs.shape[1]
    south_rows = truncate(zonal[:, :, :band_rows], cutoffs[0])
    north_rows = truncate(zonal[:, :, lat_total - band_rows:], jnp.flip(cutoffs[1], 0))
    zonal = jnp.concatenate([south_rows, zonal[:, :, band_rows:lat_total - band_rows], north_rows], axis=2)
    merid_fluxes = interface_flux(lat_level, lat_level[2:3], 2, lat_total) * face_cos
    meridional = (merid_fluxes[:, :, :-1] - merid_fluxes[:, :, 1:]) / centre_cos
    north_slope = 0.5 * (phi_lat[:, 4:lat_total + 4] - phi_lat[:, 2:lat_total + 2])
    turning = coriolis_scale * centre_sin
    flux_tendency = zonal + meridional
    east_wind = flux_tendency[1] + turning * fields[2]
    north_wind = flux_tendency[2] - turning * fields[1] - north_slope
    flux_tendency = jnp.concatenate([flux_tendency[:1], east_wind[None], north_wind[None], flux_tendency[3:]], axis=0)
    return fields + time_step * flux_tendency


def substep(state, cutoffs):
    field_count, level_count, lon_total, lat_total = state.shape
    half_turn = lon_total // 2
    wind_flip = jnp.array(wind_sign, dtype=jnp.float32)[:, None, None, None]
    south_rim = jnp.roll(jnp.flip(state[..., 0:3], 3), half_turn, axis=2) * wind_flip
    north_rim = jnp.roll(jnp.flip(state[..., lat_total - 3:], 3), half_turn, axis=2) * wind_flip
    lat_padded = jnp.concatenate([south_rim, state, north_rim], axis=3)
    lon_padded = jnp.concatenate([state[:, :, lon_total - 3:], state, state[:, :, :3]], axis=2)
    phi_lon = geopotential(lon_padded)
    phi_lat = geopotential(lat_padded)
    geometry = latitude_rows(0, lat_total, lat_total)

    def one_level(packed):
        lon_level, lat_level, fields, level_lon, level_lat = packed
        return level_update(lon_level, lat_level, fields, level_lon, level_lat, geometry, cutoffs)

    result = lax.map(one_level, (jnp.swapaxes(lon_padded, 0, 1), jnp.swapaxes(lat_padded, 0, 1), jnp.swapaxes(state, 0, 1), phi_lon, phi_lat))
    return jnp.swapaxes(result, 0, 1)


def reference(state, cutoffs):
    for substep_index in range(SUBSTEPS):
        state = substep(state, cutoffs)
    return state
```

```python
import functools

import jax
import jax.numpy as jnp
import numpy as np
from jax import lax
from jax.experimental import pallas as pl
from jax.experimental.pallas import tpu as pltpu
from jax.sharding import PartitionSpec as P

SUBSTEPS = 2


time_step = 0.5
gravity_scale = 0.25
coriolis_scale = 0.5
wind_sign = (1.0, -1.0, -1.0, 1.0, 1.0)
highest = lax.Precision.HIGHEST
inner_factor = 64
MESH = pl.DeviceIdType.MESH


def passed_along(value, axis, steps):
    count = lax.axis_size(axis)
    pairs = [(source, (source + steps) % count) for source in range(count)]
    return lax.ppermute(value, axis, pairs)


def extended(array, sides, width, wrap):
    for axis, dim in sides:
        peers, length = (lax.axis_size(axis), array.shape[dim])
        up = [(i, (i + 1) % peers) for i in range(peers if wrap else peers - 1)]
        down = [(j, i) for i, j in up]
        last = lax.slice_in_dim(array, length - width, length, axis=dim)
        initial = lax.slice_in_dim(array, 0, width, axis=dim)
        before = lax.ppermute(last, axis, up)
        after = lax.ppermute(initial, axis, down)
        array = jnp.concatenate([before, array, after], axis=dim)
    return array


def interface_flux(halo_padded, transported_field, advection_axis, extent_length):

    def shifted(offset):
        return lax.slice_in_dim(
            halo_padded, offset, offset + extent_length + 1, axis=advection_axis
        )

    far_west, mid_west, near_west, centre, near_east, far_east = [
        shifted(offset) for offset in range(6)
    ]
    interface_velocity = 0.5 * (
        lax.slice_in_dim(transported_field, 2, extent_length + 3, axis=advection_axis)
        + lax.slice_in_dim(transported_field, 3, extent_length + 4, axis=advection_axis)
    )
    central = (
        37.0 * (centre + near_west) - 8.0 * (near_east + mid_west) + (far_east + far_west)
    ) / 60.0
    upwind = (
        far_east - far_west - 5.0 * (near_east - mid_west) + 10.0 * (centre - near_west)
    ) / 60.0
    return interface_velocity * central - jnp.abs(interface_velocity) * upwind


def latitude_rows(first_row, row_count, total_rows):
    centres = (first_row + jnp.arange(row_count, dtype=jnp.int32)).astype(jnp.float32) + 0.5
    centre_cos = jnp.sin(centres * (jnp.pi / total_rows))
    centre_sin = -jnp.cos(centres * (jnp.pi / total_rows))
    faces = first_row + jnp.arange(row_count + 1, dtype=jnp.int32)
    face_cos = jnp.sin(
        jnp.minimum(faces, total_rows - faces).astype(jnp.float32) * (jnp.pi / total_rows)
    )
    return (centre_cos, centre_sin, face_cos)


def geopotential(fields):
    layer_mass = fields[0] * fields[3]
    return gravity_scale * jnp.flip(jnp.cumsum(jnp.flip(layer_mass, 0), axis=0), 0)


def zonal_tendency(lon_padded, centre_cos):
    lon_cells = lon_padded.shape[2] - 6
    face_fluxes = interface_flux(lon_padded, lon_padded[1:2], 2, lon_cells)
    zonal = face_fluxes[:, :, :-1] - face_fluxes[:, :, 1:]
    height = geopotential(lon_padded)
    height_slope = 0.5 * (height[:, 4 : lon_cells + 4] - height[:, 2 : lon_cells + 2])
    zonal = jnp.concatenate([zonal[:1], zonal[1:2] - height_slope[None], zonal[2:]], axis=0)
    return zonal / centre_cos


def phase_table(first, second, modulus, total):
    angle = (first[:, None] * second[None, :] % modulus).astype(jnp.float32) * (
        2.0 * jnp.pi / total
    )
    return (jnp.cos(angle), jnp.sin(angle))


def truncate_rows(rows, row_limit, lon_total):
    row_count = rows.shape[0]
    outer = lon_total // inner_factor
    outer_index = jnp.arange(outer, dtype=jnp.int32)
    inner_index = jnp.arange(inner_factor, dtype=jnp.int32)
    outer_cos, outer_sin = phase_table(outer_index, outer_index, outer, outer)
    twist_cos, twist_sin = phase_table(outer_index, inner_index, lon_total, lon_total)
    inner_cos, inner_sin = phase_table(inner_index, inner_index, inner_factor, inner_factor)
    folded = rows.reshape(row_count, outer, inner_factor)
    first_re = jnp.einsum("rpq,pk->rkq", folded, outer_cos, precision=highest)
    first_im = -jnp.einsum("rpq,pk->rkq", folded, outer_sin, precision=highest)
    turned_re = first_re * twist_cos + first_im * twist_sin
    turned_im = first_im * twist_cos - first_re * twist_sin
    spec_re = jnp.einsum("rkq,qj->rkj", turned_re, inner_cos, precision=highest) + jnp.einsum(
        "rkq,qj->rkj", turned_im, inner_sin, precision=highest
    )
    spec_im = jnp.einsum("rkq,qj->rkj", turned_im, inner_cos, precision=highest) - jnp.einsum(
        "rkq,qj->rkj", turned_re, inner_sin, precision=highest
    )
    wave = outer_index[:, None] + outer * inner_index[None, :]
    wave = jnp.minimum(wave, lon_total - wave).astype(jnp.float32)
    kept = wave[None, :, :] <= row_limit[:, None, None]
    spec_re = jnp.where(kept, spec_re, 0.0)
    spec_im = jnp.where(kept, spec_im, 0.0)
    back_re = jnp.einsum("rkj,qj->rkq", spec_re, inner_cos, precision=highest) - jnp.einsum(
        "rkj,qj->rkq", spec_im, inner_sin, precision=highest
    )
    back_im = jnp.einsum("rkj,qj->rkq", spec_re, inner_sin, precision=highest) + jnp.einsum(
        "rkj,qj->rkq", spec_im, inner_cos, precision=highest
    )
    untwist_re = back_re * twist_cos - back_im * twist_sin
    untwist_im = back_re * twist_sin + back_im * twist_cos
    result = jnp.einsum("rkq,pk->rpq", untwist_re, outer_cos, precision=highest) - jnp.einsum(
        "rkq,pk->rpq", untwist_im, outer_sin, precision=highest
    )
    return result.reshape(row_count, lon_total) / lon_total


def crossing_rims(state, is_south, is_north):
    lat_cells = state.shape[3]
    lon_count = lax.axis_size("lon")
    wind_flip = jnp.array(wind_sign, dtype=jnp.float32)[:, None, None, None]
    pole_rows = jnp.where(is_south, state[..., 0:2], state[..., lat_cells - 2 :])
    partner = passed_along(pole_rows, "lon", lon_count // 2) * wind_flip
    lat_halo = extended(state, (("lat", 3),), 3, False)
    south_rim = jnp.where(
        is_south,
        jnp.concatenate([lat_halo[..., 0:1], partner[..., 1:2], partner[..., 0:1]], axis=3),
        lat_halo[..., 0:3],
    )
    north_rim = jnp.where(
        is_north,
        jnp.concatenate(
            [partner[..., 1:2], partner[..., 0:1], lat_halo[..., lat_cells + 5 :]], axis=3
        ),
        lat_halo[..., lat_cells + 3 :],
    )
    return jnp.concatenate([south_rim, state, north_rim], axis=3)


def advance(state, geometry, cutoff_row, is_south, is_north):
    centre_cos, centre_sin, face_cos = geometry
    field_count, level_count, lon_cells, lat_cells = state.shape
    lon_count = lax.axis_size("lon")
    lon_total = lon_cells * lon_count
    lon_padded = extended(state, (("lon", 2),), 3, True)
    zonal = zonal_tendency(lon_padded, centre_cos)
    row_block = jnp.transpose(zonal, (0, 1, 3, 2)).reshape(lon_count, -1, lon_cells)
    row_limits = jnp.broadcast_to(cutoff_row, (field_count, level_count, lat_cells)).reshape(
        lon_count, -1, 1
    )
    values = lax.all_to_all(row_block, "lon", split_axis=0, concat_axis=2, tiled=True)
    limits = lax.all_to_all(row_limits, "lon", split_axis=0, concat_axis=2, tiled=True)
    spread = truncate_rows(values[0], limits[0, :, 0], lon_total)[None]
    returned = lax.all_to_all(spread, "lon", split_axis=2, concat_axis=0, tiled=True)
    filtered = jnp.transpose(
        returned.reshape(field_count, level_count, lat_cells, lon_cells), (0, 1, 3, 2)
    )
    zonal = jnp.where(jnp.logical_or(is_south, is_north), filtered, zonal)
    lat_padded = crossing_rims(state, is_south, is_north)
    merid_fluxes = interface_flux(lat_padded, lat_padded[2:3], 3, lat_cells) * face_cos
    meridional = (merid_fluxes[..., :-1] - merid_fluxes[..., 1:]) / centre_cos
    height = geopotential(lat_padded)
    north_slope = 0.5 * (height[..., 4 : lat_cells + 4] - height[..., 2 : lat_cells + 2])
    turning = coriolis_scale * centre_sin
    flux_tendency = zonal + meridional
    east_wind = flux_tendency[1] + turning * state[2]
    north_wind = flux_tendency[2] - turning * state[1] - north_slope
    flux_tendency = jnp.concatenate(
        [flux_tendency[:1], east_wind[None], north_wind[None], flux_tendency[3:]], axis=0
    )
    return state + time_step * flux_tendency


def circle_tables(count, width, lanes):
    total = count * width
    inner = np.arange(width)
    angle = 2.0 * np.pi * (inner[:, None] * inner[None, :] % width) / width
    table = np.zeros((lanes, 2 * lanes), np.float32)
    table[:width, :width] = np.cos(angle)
    table[:width, lanes : lanes + width] = np.sin(angle)
    high = table.astype(jnp.bfloat16)
    low = (table - high.astype(np.float32)).astype(jnp.bfloat16)
    outer = np.arange(count // 2 + 1)
    turn = 2.0 * np.pi * (outer[:, None] * np.arange(lanes)[None, :] % total) / total
    twist = np.stack([np.cos(turn), np.sin(turn)]).astype(np.float32)
    return high, low, twist


def circle_kernel(
    count, width, bands, x_ref, geo_ref, twist_ref, high_ref, low_ref, out_ref,
    outgoing, states, incoming, filtered, carrier, spectrum, halo_out, halo_in,
    first_send, first_recv, last_send, last_recv, halo_send, halo_recv,
):
    fields = x_ref.shape[0]
    lanes = outgoing.shape[2]
    rows = geo_ref.shape[1]
    half = count // 2
    total = count * width
    me = lax.axis_index("lon")
    lat = lax.axis_index("lat")
    even = lax.rem(lat, 2) == 0

    def band_of(device):
        return jnp.where(even, device, count - 1 - device)

    band = band_of(me)
    at_south = jnp.logical_and(band == 0, lat == 0)
    at_north = jnp.logical_and(band == count - 1, lat == bands - 1)
    step = jnp.where(even, 1, -1)
    south_lon = jnp.where(band == 0, me, me - step)
    south_lat = jnp.where(band == 0, lat - 1, lat)
    north_lon = jnp.where(band == count - 1, me, me + step)
    north_lat = jnp.where(band == count - 1, lat + 1, lat)
    lane = lax.broadcasted_iota(jnp.int32, (rows, lanes), 1)
    inside = lane < width

    barrier = pltpu.get_barrier_semaphore()

    def greet(offset, carry):
        peer = lax.rem(me + offset, count)
        pl.semaphore_signal(barrier, inc=1, device_id={"lon": peer, "lat": lat}, device_id_type=MESH)
        return carry

    lax.fori_loop(1, count, greet, 0)
    crosses_south = jnp.logical_and(band == 0, lat > 0)
    crosses_north = jnp.logical_and(band == count - 1, lat < bands - 1)

    @pl.when(crosses_south)
    def _():
        pl.semaphore_signal(barrier, inc=1, device_id={"lon": me, "lat": lat - 1}, device_id_type=MESH)

    @pl.when(crosses_north)
    def _():
        pl.semaphore_signal(barrier, inc=1, device_id={"lon": me, "lat": lat + 1}, device_id_type=MESH)

    def first_copy(field, peer, slot):
        start = pl.multiple_of(band_of(peer) * rows, rows)
        return pltpu.make_async_remote_copy(
            src_ref=outgoing.at[field, pl.ds(start, rows), :],
            dst_ref=states.at[0, field, slot, pl.ds(8, rows), :],
            send_sem=first_send.at[field, peer],
            recv_sem=first_recv.at[field, slot],
            device_id={"lon": peer, "lat": lat},
            device_id_type=MESH,
        )

    def last_copy(field, peer, owner):
        start = pl.multiple_of(band_of(owner) * rows, rows)
        return pltpu.make_async_remote_copy(
            src_ref=states.at[2, field, peer, pl.ds(8, rows), :],
            dst_ref=incoming.at[field, pl.ds(start, rows), :],
            send_sem=last_send.at[field, peer],
            recv_sem=last_recv.at[field, owner],
            device_id={"lon": peer, "lat": lat},
            device_id_type=MESH,
        )

    def over_peers(action):
        def one(offset, carry):
            action(lax.rem(me + offset, count))
            return carry

        lax.fori_loop(1, count, one, 0)

    def halo_copy(turn, side, field):
        return pltpu.make_async_remote_copy(
            src_ref=halo_out.at[turn, side, field],
            dst_ref=halo_in.at[turn, 1 - side, field],
            send_sem=halo_send.at[turn, side, field],
            recv_sem=halo_recv.at[turn, 1 - side, field],
            device_id={
                "lon": south_lon if side == 0 else north_lon,
                "lat": south_lat if side == 0 else north_lat,
            },
            device_id_type=MESH,
        )

    def send_halo(turn, field):
        for p in range(count):
            halo_out[turn, 0, field, 3 * p : 3 * p + 3, :] = states[turn, field, p, 8:11, :]
            halo_out[turn, 1, field, 3 * p : 3 * p + 3, :] = states[turn, field, p, rows + 5 : rows + 8, :]

        @pl.when(jnp.logical_not(at_south))
        def _():
            halo_copy(turn, 0, field).start()

        @pl.when(jnp.logical_not(at_north))
        def _():
            halo_copy(turn, 1, field).start()

    def take_halo(turn, field):
        sign = jnp.where(jnp.logical_or(field == 1, field == 2), -1.0, 1.0)

        @pl.when(jnp.logical_not(at_south))
        def _():
            copy = halo_copy(turn, 0, field)
            copy.wait_send()
            arrival = pltpu.make_async_remote_copy(
                src_ref=halo_out.at[turn, 0, field],
                dst_ref=halo_in.at[turn, 0, field],
                send_sem=halo_send.at[turn, 0, field],
                recv_sem=halo_recv.at[turn, 0, field],
                device_id={"lon": south_lon, "lat": south_lat},
                device_id_type=MESH,
            )
            arrival.wait_recv()
            for p in range(count):
                states[turn, field, p, 5:8, :] = halo_in[turn, 0, field, 3 * p : 3 * p + 3, :]

        @pl.when(at_south)
        def _():
            for p in range(count):
                for m in range(3):
                    states[turn, field, p, 7 - m : 8 - m, :] = (
                        sign * states[turn, field, (p + half) % count, 8 + m : 9 + m, :]
                    )

        @pl.when(jnp.logical_not(at_north))
        def _():
            copy = halo_copy(turn, 1, field)
            copy.wait_send()
            arrival = pltpu.make_async_remote_copy(
                src_ref=halo_out.at[turn, 1, field],
                dst_ref=halo_in.at[turn, 1, field],
                send_sem=halo_send.at[turn, 1, field],
                recv_sem=halo_recv.at[turn, 1, field],
                device_id={"lon": north_lon, "lat": north_lat},
                device_id_type=MESH,
            )
            arrival.wait_recv()
            for p in range(count):
                states[turn, field, p, rows + 8 : rows + 11, :] = halo_in[
                    turn, 1, field, 3 * p : 3 * p + 3, :
                ]

        @pl.when(at_north)
        def _():
            for p in range(count):
                for m in range(3):
                    states[turn, field, p, rows + 8 + m : rows + 9 + m, :] = (
                        sign
                        * states[turn, field, (p + half) % count, rows + 7 - m : rows + 8 - m, :]
                    )

    def arrive(field):
        def one(peer):
            first_copy(field, peer, peer).wait_recv()

        over_peers(one)
        send_halo(0, field)

    def wrapped(turn, field, p):
        east = lax.rem(p + 1, count)
        west = lax.rem(p + count - 1, count)
        core = states[turn, field, p, 8 : 8 + rows, :]
        after = pltpu.roll(states[turn, field, east, 8 : 8 + rows, :], width, 1)
        before = pltpu.roll(states[turn, field, west, 8 : 8 + rows, :], lanes - width, 1)
        middle = width + (lanes - width) // 2
        return jnp.where(inside, core, jnp.where(lane < middle, after, before))

    def moved(value, offset):
        return pltpu.roll(value, (-offset) % lanes, 1)

    def face_flux(carrying, m3, m2, m1, c0, p1, p2):
        central = 37.0 * (c0 + m1) - 8.0 * (p1 + m2) + (p2 + m3)
        upwind = (p2 - m3) - 5.0 * (p1 - m2) + 10.0 * (c0 - m1)
        return carrying * central - jnp.abs(carrying) * upwind

    def over_tiles(action, group=2):
        def one(block, carry):
            for inner in range(group):
                action(block * group + inner)
            return carry

        lax.fori_loop(0, count // group, one, 0)

    chunks = [slice(128 * c, 128 * c + 128) for c in range(lanes // 128)]
    waves = half + 1
    block = waves * rows

    def product():
        value = spectrum[...]
        high = value.astype(jnp.bfloat16)
        low = (value - high.astype(jnp.float32)).astype(jnp.bfloat16)
        weights = high_ref[...]
        result = jnp.dot(high, weights, preferred_element_type=jnp.float32)
        result += jnp.dot(low, weights, preferred_element_type=jnp.float32)
        return result + jnp.dot(high, low_ref[...], preferred_element_type=jnp.float32)

    def cos_of(k, p):
        return float(np.cos(2.0 * np.pi * (k * p % count) / count))

    def sin_of(k, p):
        return float(np.sin(2.0 * np.pi * (k * p % count) / count))

    def combined(terms):
        value = None
        for factor, term in terms:
            if abs(factor) < 1e-9:
                continue
            if abs(abs(factor) - 1.0) < 1e-9:
                scaled = term
            else:
                scaled = abs(factor) * term
            if value is None:
                value = scaled if factor > 0 else -scaled
            elif factor > 0:
                value = value + scaled
            else:
                value = value - scaled
        return value

    def truncate(field):
        for cut in chunks:
            z = [filtered[field, p, :, cut] for p in range(count)]
            sums = [z[0]] + [z[p] + z[count - p] for p in range(1, half)] + [z[half]]
            gaps = [None] + [z[p] - z[count - p] for p in range(1, half)]
            for k in range(waves):
                cosine = twist_ref[0, k : k + 1, cut]
                sine = twist_ref[1, k : k + 1, cut]
                real = combined([(cos_of(k, p), sums[p]) for p in range(half + 1)])
                imag = combined([(-sin_of(k, p), gaps[p]) for p in range(1, half)])
                if imag is None:
                    turned_re, turned_im = real * cosine, -(real * sine)
                else:
                    turned_re = real * cosine + imag * sine
                    turned_im = imag * cosine - real * sine
                spectrum[k * rows : (k + 1) * rows, cut] = turned_re
                spectrum[block + k * rows : block + (k + 1) * rows, cut] = turned_im
        result = product()
        limit = geo_ref[4]
        for k in range(waves):
            top = slice(k * rows, (k + 1) * rows)
            low = slice(block + k * rows, block + (k + 1) * rows)
            wave = k + count * lane
            wave = jnp.minimum(wave, total - wave).astype(jnp.float32)
            kept = wave <= limit
            spectrum[top, :] = jnp.where(kept, result[top, :lanes] + result[low, lanes:], 0.0)
            spectrum[low, :] = jnp.where(kept, result[low, :lanes] - result[top, lanes:], 0.0)
        result = product()
        scale = 1.0 / total
        for c, cut in enumerate(chunks):
            sin_cut = slice(lanes + 128 * c, lanes + 128 * c + 128)
            reals, imags = [], []
            for k in range(waves):
                top = slice(k * rows, (k + 1) * rows)
                low = slice(block + k * rows, block + (k + 1) * rows)
                factor = scale if k in (0, half) else 2.0 * scale
                cosine = twist_ref[0, k : k + 1, cut] * factor
                sine = twist_ref[1, k : k + 1, cut] * factor
                back_re = result[top, cut] - result[low, sin_cut]
                back_im = result[top, sin_cut] + result[low, cut]
                reals.append(back_re * cosine - back_im * sine)
                imags.append(back_im * cosine + back_re * sine)
            for p in range(half + 1):
                even_part = combined([(cos_of(k, p), reals[k]) for k in range(waves)])
                odd_part = combined([(sin_of(k, p), imags[k]) for k in range(1, half)])
                if odd_part is None:
                    filtered[field, p, :, cut] = even_part
                else:
                    filtered[field, p, :, cut] = even_part - odd_part
                    filtered[field, count - p, :, cut] = even_part + odd_part

    for index, field in enumerate((1, 0, 3, 4, 2)):
        source = jnp.concatenate(
            [x_ref[field], jnp.zeros((lanes - width, x_ref.shape[2]), jnp.float32)], axis=0
        )
        outgoing[field] = source.T
        if index == 0:
            expected = count - 1 + crosses_south.astype(jnp.int32) + crosses_north.astype(jnp.int32)
            pl.semaphore_wait(barrier, expected)

        def send(peer, field=field):
            first_copy(field, peer, me).start()

        over_peers(send)
        own = pl.multiple_of(band * rows, rows)
        states[0, field, me, 8 : 8 + rows, :] = outgoing[field, pl.ds(own, rows), :]

    def substep(turn, carry):
        @pl.when(turn == 0)
        def _():
            arrive(1)

        def make_carrier(p):
            wind = wrapped(turn, 1, p)
            carrier[p] = (wind + moved(wind, -1)) * (1.0 / 120.0)

        over_tiles(make_carrier)

        def along_circles(index, inner_carry):
            field = lax.rem(index * 3, fields)

            @pl.when(jnp.logical_and(turn == 0, field != 1))
            def _():
                arrive(field)

            def one(p):
                value = wrapped(turn, field, p)
                flux = face_flux(
                    carrier[p], moved(value, -3), moved(value, -2), moved(value, -1), value,
                    moved(value, 1), moved(value, 2),
                )
                zonal = (flux - moved(flux, 1)) * geo_ref[0]
                filtered[field, p] = jnp.where(inside, zonal, 0.0)

            over_tiles(one)

            @pl.when(field == 1)
            def _():
                def slope(p):
                    height = wrapped(turn, 0, p) * wrapped(turn, 3, p)
                    drop = (moved(height, 1) - moved(height, -1)) * (0.5 * gravity_scale)
                    filtered[field, p] = filtered[field, p] - jnp.where(inside, drop * geo_ref[0], 0.0)

                over_tiles(slope)

            truncate(field)
            return inner_carry

        lax.fori_loop(0, fields, along_circles, 0)

        def gather_halo(field, inner_carry):
            take_halo(turn, field)
            return inner_carry

        lax.fori_loop(0, fields, gather_halo, 0)

        def across_rows(field, inner_carry):
            def one(p):
                def at(which, offset):
                    return states[turn, which, p, 8 + offset : 8 + offset + rows, :]

                below, here, above = at(2, -1), at(2, 0), at(2, 1)
                around = [at(field, offset) for offset in range(-3, 4)]
                lower = face_flux((below + here) * (1.0 / 120.0), *around[:6])
                upper = face_flux((here + above) * (1.0 / 120.0), *around[1:])
                change = filtered[field, p] + (lower * geo_ref[1] - upper * geo_ref[2])
                states[turn + 1, field, p, 8 : 8 + rows, :] = around[3] + time_step * change

            over_tiles(one)

            @pl.when(field == 1)
            def _():
                def turning(p):
                    old = states[turn + 1, field, p, 8 : 8 + rows, :]
                    wind = states[turn, 2, p, 8 : 8 + rows, :]
                    states[turn + 1, field, p, 8 : 8 + rows, :] = old + time_step * (geo_ref[3] * wind)

                over_tiles(turning)

            @pl.when(field == 2)
            def _():
                def turning(p):
                    old = states[turn + 1, field, p, 8 : 8 + rows, :]
                    wind = states[turn, 1, p, 8 : 8 + rows, :]
                    upper = states[turn, 0, p, 9 : 9 + rows, :] * states[turn, 3, p, 9 : 9 + rows, :]
                    lower = states[turn, 0, p, 7 : 7 + rows, :] * states[turn, 3, p, 7 : 7 + rows, :]
                    slope = (upper - lower) * (0.5 * gravity_scale)
                    states[turn + 1, field, p, 8 : 8 + rows, :] = old - time_step * (
                        geo_ref[3] * wind + slope
                    )

                over_tiles(turning)

            @pl.when(turn == 0)
            def _():
                send_halo(1, field)

            @pl.when(turn == 1)
            def _():
                over_peers(lambda peer: last_copy(field, peer, me).start())

            return inner_carry

        lax.fori_loop(0, fields, across_rows, 0)
        return carry

    lax.fori_loop(0, SUBSTEPS, substep, 0)

    own = pl.multiple_of(band * rows, rows)
    for field in range(fields):
        incoming[field, pl.ds(own, rows), :] = states[2, field, me, 8 : 8 + rows, :]

        def arrived(peer, field=field):
            last_copy(field, peer, peer).wait_recv()

        over_peers(arrived)
        out_ref[field] = incoming[field].T[:width]

    for field in range(fields):

        def sent(peer, field=field):
            first_copy(field, peer, me).wait_send()
            last_copy(field, peer, me).wait_send()

        over_peers(sent)


def circle_advance(state, cutoff_row, lon_count, lat_count):
    fields, _, width, lat_cells = state.shape
    rows = lat_cells // lon_count
    lanes = padded_lanes(width)
    half = lon_count // 2
    me, lat = lax.axis_index("lon"), lax.axis_index("lat")
    band = jnp.where(lat % 2 == 0, me, lon_count - 1 - me)
    centre_cos, centre_sin, face_cos = latitude_rows(
        lat * lat_cells + band * rows, rows, lat_cells * lat_count
    )
    limit = lax.dynamic_slice(cutoff_row, (band * rows,), (rows,))
    table = jnp.stack([
        1.0 / centre_cos, face_cos[:-1] / centre_cos, face_cos[1:] / centre_cos,
        coriolis_scale * centre_sin, limit,
    ])
    geometry = jnp.broadcast_to(table[:, :, None], (5, rows, lanes))
    high, low, twist = circle_tables(lon_count, width, lanes)
    vmem = pl.BlockSpec(memory_space=pltpu.VMEM)
    dma = pltpu.SemaphoreType.DMA
    f32 = jnp.float32
    result = pl.pallas_call(
        functools.partial(circle_kernel, lon_count, width, lat_count),
        out_shape=jax.ShapeDtypeStruct((fields, width, lat_cells), f32),
        in_specs=[vmem] * 5,
        out_specs=vmem,
        scratch_shapes=[
            pltpu.VMEM((fields, lat_cells, lanes), f32),
            pltpu.VMEM((3, fields, lon_count, rows + 16, lanes), f32),
            pltpu.VMEM((fields, lat_cells, lanes), f32),
            pltpu.VMEM((fields, lon_count, rows, lanes), f32),
            pltpu.VMEM((lon_count, rows, lanes), f32),
            pltpu.VMEM((2 * (half + 1) * rows, lanes), f32),
            pltpu.VMEM((2, 2, fields, 3 * lon_count, lanes), f32),
            pltpu.VMEM((2, 2, fields, 3 * lon_count, lanes), f32),
            dma((fields, lon_count)), dma((fields, lon_count)),
            dma((fields, lon_count)), dma((fields, lon_count)),
            dma((2, 2, fields)), dma((2, 2, fields)),
        ],
        compiler_params=pltpu.CompilerParams(
            collective_id=0, has_side_effects=True, vmem_limit_bytes=48 * 1024 * 1024
        ),
    )(state[:, 0], geometry, twist, high, low)
    return result[:, None]


def padded_lanes(width):
    return -(-(width + 6) // 128) * 128


def fits_circles(state, lon_count, lat_count):
    fields, levels, width, lat_cells = state.shape
    return (
        fields == 5 and levels == 1 and width % 8 == 0 and lat_cells % 128 == 0
        and lon_count % 4 == 0 and lat_cells == 8 * lon_count and lat_count > 1
    )


def shards(state, cutoffs):
    lat_index = lax.axis_index("lat")
    lat_count = lax.axis_size("lat")
    lon_count = lax.axis_size("lon")
    lat_cells = state.shape[3]
    is_south = lat_index == 0
    is_north = lat_index == lat_count - 1
    if fits_circles(state, lon_count, lat_count):
        unfiltered = lon_count * state.shape[2]
        north_row = jnp.where(is_north, jnp.flip(cutoffs[1], 0), unfiltered)
        cutoff_row = jnp.where(is_south, cutoffs[0], north_row).astype(jnp.float32)
        return circle_advance(state, cutoff_row, lon_count, lat_count)
    geometry = latitude_rows(lat_index * lat_cells, lat_cells, lat_cells * lat_count)
    north_row = jnp.where(is_north, jnp.flip(cutoffs[1], 0), -1)
    cutoff_row = jnp.where(is_south, cutoffs[0], north_row).astype(jnp.float32)
    for substep_index in range(SUBSTEPS):
        state = advance(state, geometry, cutoff_row, is_south, is_north)
    return state


def solution(mesh):
    return jax.shard_map(
        shards,
        mesh=mesh,
        in_specs=(P(None, None, "lon", "lat"), P()),
        out_specs=P(None, None, "lon", "lat"),
        check_vma=False,
    )
```

```python
import functools

import jax
import jax.numpy as jnp
import numpy as np
from jax import lax
from jax.experimental import pallas as pl
from jax.experimental.pallas import tpu as pltpu
from jax.sharding import PartitionSpec as P

SUBSTEPS = 2


time_step = 0.5
gravity_scale = 0.25
coriolis_scale = 0.5
wind_sign = (1.0, -1.0, -1.0, 1.0, 1.0)
highest = lax.Precision.HIGHEST
inner_factor = 64
MESH = pl.DeviceIdType.MESH


def passed_along(value, axis, steps):
    count = lax.axis_size(axis)
    pairs = [(source, (source + steps) % count) for source in range(count)]
    return lax.ppermute(value, axis, pairs)


def extended(array, sides, width, wrap):
    for axis, dim in sides:
        peers, length = (lax.axis_size(axis), array.shape[dim])
        up = [(i, (i + 1) % peers) for i in range(peers if wrap else peers - 1)]
        down = [(j, i) for i, j in up]
        last = lax.slice_in_dim(array, length - width, length, axis=dim)
        initial = lax.slice_in_dim(array, 0, width, axis=dim)
        before = lax.ppermute(last, axis, up)
        after = lax.ppermute(initial, axis, down)
        array = jnp.concatenate([before, array, after], axis=dim)
    return array


def interface_flux(halo_padded, transported_field, advection_axis, extent_length):

    def shifted(offset):
        return lax.slice_in_dim(
            halo_padded, offset, offset + extent_length + 1, axis=advection_axis
        )

    far_west, mid_west, near_west, centre, near_east, far_east = [
        shifted(offset) for offset in range(6)
    ]
    interface_velocity = 0.5 * (
        lax.slice_in_dim(transported_field, 2, extent_length + 3, axis=advection_axis)
        + lax.slice_in_dim(transported_field, 3, extent_length + 4, axis=advection_axis)
    )
    central = (
        37.0 * (centre + near_west) - 8.0 * (near_east + mid_west) + (far_east + far_west)
    ) / 60.0
    upwind = (
        far_east - far_west - 5.0 * (near_east - mid_west) + 10.0 * (centre - near_west)
    ) / 60.0
    return interface_velocity * central - jnp.abs(interface_velocity) * upwind


def latitude_rows(first_row, row_count, total_rows):
    centres = (first_row + jnp.arange(row_count, dtype=jnp.int32)).astype(jnp.float32) + 0.5
    centre_cos = jnp.sin(centres * (jnp.pi / total_rows))
    centre_sin = -jnp.cos(centres * (jnp.pi / total_rows))
    faces = first_row + jnp.arange(row_count + 1, dtype=jnp.int32)
    face_cos = jnp.sin(
        jnp.minimum(faces, total_rows - faces).astype(jnp.float32) * (jnp.pi / total_rows)
    )
    return (centre_cos, centre_sin, face_cos)


def geopotential(fields):
    layer_mass = fields[0] * fields[3]
    return gravity_scale * jnp.flip(jnp.cumsum(jnp.flip(layer_mass, 0), axis=0), 0)


def zonal_tendency(lon_padded, centre_cos):
    lon_cells = lon_padded.shape[2] - 6
    face_fluxes = interface_flux(lon_padded, lon_padded[1:2], 2, lon_cells)
    zonal = face_fluxes[:, :, :-1] - face_fluxes[:, :, 1:]
    height = geopotential(lon_padded)
    height_slope = 0.5 * (height[:, 4 : lon_cells + 4] - height[:, 2 : lon_cells + 2])
    zonal = jnp.concatenate([zonal[:1], zonal[1:2] - height_slope[None], zonal[2:]], axis=0)
    return zonal / centre_cos


def phase_table(first, second, modulus, total):
    angle = (first[:, None] * second[None, :] % modulus).astype(jnp.float32) * (
        2.0 * jnp.pi / total
    )
    return (jnp.cos(angle), jnp.sin(angle))


def truncate_rows(rows, row_limit, lon_total):
    row_count = rows.shape[0]
    outer = lon_total // inner_factor
    outer_index = jnp.arange(outer, dtype=jnp.int32)
    inner_index = jnp.arange(inner_factor, dtype=jnp.int32)
    outer_cos, outer_sin = phase_table(outer_index, outer_index, outer, outer)
    twist_cos, twist_sin = phase_table(outer_index, inner_index, lon_total, lon_total)
    inner_cos, inner_sin = phase_table(inner_index, inner_index, inner_factor, inner_factor)
    folded = rows.reshape(row_count, outer, inner_factor)
    first_re = jnp.einsum("rpq,pk->rkq", folded, outer_cos, precision=highest)
    first_im = -jnp.einsum("rpq,pk->rkq", folded, outer_sin, precision=highest)
    turned_re = first_re * twist_cos + first_im * twist_sin
    turned_im = first_im * twist_cos - first_re * twist_sin
    spec_re = jnp.einsum("rkq,qj->rkj", turned_re, inner_cos, precision=highest) + jnp.einsum(
        "rkq,qj->rkj", turned_im, inner_sin, precision=highest
    )
    spec_im = jnp.einsum("rkq,qj->rkj", turned_im, inner_cos, precision=highest) - jnp.einsum(
        "rkq,qj->rkj", turned_re, inner_sin, precision=highest
    )
    wave = outer_index[:, None] + outer * inner_index[None, :]
    wave = jnp.minimum(wave, lon_total - wave).astype(jnp.float32)
    kept = wave[None, :, :] <= row_limit[:, None, None]
    spec_re = jnp.where(kept, spec_re, 0.0)
    spec_im = jnp.where(kept, spec_im, 0.0)
    back_re = jnp.einsum("rkj,qj->rkq", spec_re, inner_cos, precision=highest) - jnp.einsum(
        "rkj,qj->rkq", spec_im, inner_sin, precision=highest
    )
    back_im = jnp.einsum("rkj,qj->rkq", spec_re, inner_sin, precision=highest) + jnp.einsum(
        "rkj,qj->rkq", spec_im, inner_cos, precision=highest
    )
    untwist_re = back_re * twist_cos - back_im * twist_sin
    untwist_im = back_re * twist_sin + back_im * twist_cos
    result = jnp.einsum("rkq,pk->rpq", untwist_re, outer_cos, precision=highest) - jnp.einsum(
        "rkq,pk->rpq", untwist_im, outer_sin, precision=highest
    )
    return result.reshape(row_count, lon_total) / lon_total


def crossing_rims(state, is_south, is_north):
    lat_cells = state.shape[3]
    lon_count = lax.axis_size("lon")
    wind_flip = jnp.array(wind_sign, dtype=jnp.float32)[:, None, None, None]
    pole_rows = jnp.where(is_south, state[..., 0:2], state[..., lat_cells - 2 :])
    partner = passed_along(pole_rows, "lon", lon_count // 2) * wind_flip
    lat_halo = extended(state, (("lat", 3),), 3, False)
    south_rim = jnp.where(
        is_south,
        jnp.concatenate([lat_halo[..., 0:1], partner[..., 1:2], partner[..., 0:1]], axis=3),
        lat_halo[..., 0:3],
    )
    north_rim = jnp.where(
        is_north,
        jnp.concatenate(
            [partner[..., 1:2], partner[..., 0:1], lat_halo[..., lat_cells + 5 :]], axis=3
        ),
        lat_halo[..., lat_cells + 3 :],
    )
    return jnp.concatenate([south_rim, state, north_rim], axis=3)


def advance(state, geometry, cutoff_row, is_south, is_north):
    centre_cos, centre_sin, face_cos = geometry
    field_count, level_count, lon_cells, lat_cells = state.shape
    lon_count = lax.axis_size("lon")
    lon_total = lon_cells * lon_count
    lon_padded = extended(state, (("lon", 2),), 3, True)
    zonal = zonal_tendency(lon_padded, centre_cos)
    row_block = jnp.transpose(zonal, (0, 1, 3, 2)).reshape(lon_count, -1, lon_cells)
    row_limits = jnp.broadcast_to(cutoff_row, (field_count, level_count, lat_cells)).reshape(
        lon_count, -1, 1
    )
    values = lax.all_to_all(row_block, "lon", split_axis=0, concat_axis=2, tiled=True)
    limits = lax.all_to_all(row_limits, "lon", split_axis=0, concat_axis=2, tiled=True)
    spread = truncate_rows(values[0], limits[0, :, 0], lon_total)[None]
    returned = lax.all_to_all(spread, "lon", split_axis=2, concat_axis=0, tiled=True)
    filtered = jnp.transpose(
        returned.reshape(field_count, level_count, lat_cells, lon_cells), (0, 1, 3, 2)
    )
    zonal = jnp.where(jnp.logical_or(is_south, is_north), filtered, zonal)
    lat_padded = crossing_rims(state, is_south, is_north)
    merid_fluxes = interface_flux(lat_padded, lat_padded[2:3], 3, lat_cells) * face_cos
    meridional = (merid_fluxes[..., :-1] - merid_fluxes[..., 1:]) / centre_cos
    height = geopotential(lat_padded)
    north_slope = 0.5 * (height[..., 4 : lat_cells + 4] - height[..., 2 : lat_cells + 2])
    turning = coriolis_scale * centre_sin
    flux_tendency = zonal + meridional
    east_wind = flux_tendency[1] + turning * state[2]
    north_wind = flux_tendency[2] - turning * state[1] - north_slope
    flux_tendency = jnp.concatenate(
        [flux_tendency[:1], east_wind[None], north_wind[None], flux_tendency[3:]], axis=0
    )
    return state + time_step * flux_tendency


def circle_tables(count, width, lanes):
    total = count * width
    inner = np.arange(width)
    angle = 2.0 * np.pi * (inner[:, None] * inner[None, :] % width) / width
    table = np.zeros((lanes, 2 * lanes), np.float32)
    table[:width, :width] = np.cos(angle)
    table[:width, lanes : lanes + width] = np.sin(angle)
    high = table.astype(jnp.bfloat16)
    low = (table - high.astype(np.float32)).astype(jnp.bfloat16)
    outer = np.arange(count // 2 + 1)
    turn = 2.0 * np.pi * (outer[:, None] * np.arange(lanes)[None, :] % total) / total
    twist = np.stack([np.cos(turn), np.sin(turn)]).astype(np.float32)
    return high, low, twist


def circle_kernel(
    count, width, bands, x_hbm, geo_ref, twist_ref, high_hbm, low_hbm, out_ref,
    x_ref, high_ref, low_ref, x_sem, table_sem, outgoing, states, incoming, filtered, carrier, crossing, spectrum, halo_out, halo_in,
    first_send, first_recv, last_send, last_recv, halo_send, halo_recv,
):
    fields = x_ref.shape[0]
    lanes = outgoing.shape[2]
    rows = geo_ref.shape[1]
    half = count // 2
    total = count * width
    me = lax.axis_index("lon")
    lat = lax.axis_index("lat")
    even = lax.rem(lat, 2) == 0

    def band_of(device):
        return jnp.where(even, device, count - 1 - device)

    band = band_of(me)
    at_south = jnp.logical_and(band == 0, lat == 0)
    at_north = jnp.logical_and(band == count - 1, lat == bands - 1)
    step = jnp.where(even, 1, -1)
    south_lon = jnp.where(band == 0, me, me - step)
    south_lat = jnp.where(band == 0, lat - 1, lat)
    north_lon = jnp.where(band == count - 1, me, me + step)
    north_lat = jnp.where(band == count - 1, lat + 1, lat)
    lane = lax.broadcasted_iota(jnp.int32, (rows, lanes), 1)
    inside = lane < width

    barrier = pltpu.get_barrier_semaphore()

    def greet(offset, carry):
        peer = lax.rem(me + offset, count)
        pl.semaphore_signal(barrier, inc=1, device_id={"lon": peer, "lat": lat}, device_id_type=MESH)
        return carry

    lax.fori_loop(1, count, greet, 0)
    crosses_south = jnp.logical_and(band == 0, lat > 0)
    crosses_north = jnp.logical_and(band == count - 1, lat < bands - 1)

    @pl.when(crosses_south)
    def _():
        pl.semaphore_signal(barrier, inc=1, device_id={"lon": me, "lat": lat - 1}, device_id_type=MESH)

    @pl.when(crosses_north)
    def _():
        pl.semaphore_signal(barrier, inc=1, device_id={"lon": me, "lat": lat + 1}, device_id_type=MESH)

    def first_copy(field, peer, slot):
        start = pl.multiple_of(band_of(peer) * rows, rows)
        return pltpu.make_async_remote_copy(
            src_ref=outgoing.at[field, pl.ds(start, rows), :],
            dst_ref=states.at[0, field, slot, pl.ds(8, rows), :],
            send_sem=first_send.at[field, peer],
            recv_sem=first_recv.at[field, slot],
            device_id={"lon": peer, "lat": lat},
            device_id_type=MESH,
        )

    def last_copy(field, peer, owner):
        start = pl.multiple_of(band_of(owner) * rows, rows)
        return pltpu.make_async_remote_copy(
            src_ref=states.at[2, field, peer, pl.ds(8, rows), :],
            dst_ref=incoming.at[field, pl.ds(start, rows), :],
            send_sem=last_send.at[field, peer],
            recv_sem=last_recv.at[field, owner],
            device_id={"lon": peer, "lat": lat},
            device_id_type=MESH,
        )

    def over_peers(action):
        def one(offset, carry):
            action(lax.rem(me + offset, count))
            return carry

        lax.fori_loop(1, count, one, 0)

    def halo_copy(turn, side, field):
        return pltpu.make_async_remote_copy(
            src_ref=halo_out.at[turn, side, field],
            dst_ref=halo_in.at[turn, 1 - side, field],
            send_sem=halo_send.at[turn, side, field],
            recv_sem=halo_recv.at[turn, 1 - side, field],
            device_id={
                "lon": south_lon if side == 0 else north_lon,
                "lat": south_lat if side == 0 else north_lat,
            },
            device_id_type=MESH,
        )

    def send_halo(turn, field):
        for p in range(count):
            halo_out[turn, 0, field, 3 * p : 3 * p + 3, :] = states[turn, field, p, 8:11, :]
            halo_out[turn, 1, field, 3 * p : 3 * p + 3, :] = states[turn, field, p, rows + 5 : rows + 8, :]

        @pl.when(jnp.logical_not(at_south))
        def _():
            halo_copy(turn, 0, field).start()

        @pl.when(jnp.logical_not(at_north))
        def _():
            halo_copy(turn, 1, field).start()

    def take_halo(turn, field):
        sign = jnp.where(jnp.logical_or(field == 1, field == 2), -1.0, 1.0)

        @pl.when(jnp.logical_not(at_south))
        def _():
            copy = halo_copy(turn, 0, field)
            copy.wait_send()
            arrival = pltpu.make_async_remote_copy(
                src_ref=halo_out.at[turn, 0, field],
                dst_ref=halo_in.at[turn, 0, field],
                send_sem=halo_send.at[turn, 0, field],
                recv_sem=halo_recv.at[turn, 0, field],
                device_id={"lon": south_lon, "lat": south_lat},
                device_id_type=MESH,
            )
            arrival.wait_recv()
            for p in range(count):
                states[turn, field, p, 5:8, :] = halo_in[turn, 0, field, 3 * p : 3 * p + 3, :]

        @pl.when(at_south)
        def _():
            for p in range(count):
                for m in range(3):
                    states[turn, field, p, 7 - m : 8 - m, :] = (
                        sign * states[turn, field, (p + half) % count, 8 + m : 9 + m, :]
                    )

        @pl.when(jnp.logical_not(at_north))
        def _():
            copy = halo_copy(turn, 1, field)
            copy.wait_send()
            arrival = pltpu.make_async_remote_copy(
                src_ref=halo_out.at[turn, 1, field],
                dst_ref=halo_in.at[turn, 1, field],
                send_sem=halo_send.at[turn, 1, field],
                recv_sem=halo_recv.at[turn, 1, field],
                device_id={"lon": north_lon, "lat": north_lat},
                device_id_type=MESH,
            )
            arrival.wait_recv()
            for p in range(count):
                states[turn, field, p, rows + 8 : rows + 11, :] = halo_in[
                    turn, 1, field, 3 * p : 3 * p + 3, :
                ]

        @pl.when(at_north)
        def _():
            for p in range(count):
                for m in range(3):
                    states[turn, field, p, rows + 8 + m : rows + 9 + m, :] = (
                        sign
                        * states[turn, field, (p + half) % count, rows + 7 - m : rows + 8 - m, :]
                    )

    def arrive(field):
        def one(peer):
            first_copy(field, peer, peer).wait_recv()

        over_peers(one)
        send_halo(0, field)

    def wrapped(turn, field, p):
        east = lax.rem(p + 1, count)
        west = lax.rem(p + count - 1, count)
        core = states[turn, field, p, 8 : 8 + rows, :]
        after = pltpu.roll(states[turn, field, east, 8 : 8 + rows, :], width, 1)
        before = pltpu.roll(states[turn, field, west, 8 : 8 + rows, :], lanes - width, 1)
        middle = width + (lanes - width) // 2
        return jnp.where(inside, core, jnp.where(lane < middle, after, before))

    def moved(value, offset):
        return pltpu.roll(value, (-offset) % lanes, 1)

    def face_flux(carrying, m3, m2, m1, c0, p1, p2):
        central = 37.0 * (c0 + m1) - 8.0 * (p1 + m2) + (p2 + m3)
        upwind = (p2 - m3) - 5.0 * (p1 - m2) + 10.0 * (c0 - m1)
        return carrying * central - jnp.abs(carrying) * upwind

    def over_tiles(action, group=2):
        def one(block, carry):
            for inner in range(group):
                action(block * group + inner)
            return carry

        lax.fori_loop(0, count // group, one, 0)

    chunks = [slice(128 * c, 128 * c + 128) for c in range(lanes // 128)]
    waves = half + 1
    block = waves * rows

    def product():
        value = spectrum[...]
        high = value.astype(jnp.bfloat16)
        low = (value - high.astype(jnp.float32)).astype(jnp.bfloat16)
        weights = high_ref[...]
        both = jnp.dot(
            jnp.concatenate([high, low], axis=0), weights, preferred_element_type=jnp.float32
        )
        rest = jnp.dot(high, low_ref[...], preferred_element_type=jnp.float32)
        return both[: 2 * block] + both[2 * block :] + rest

    def cos_of(k, p):
        return float(np.cos(2.0 * np.pi * (k * p % count) / count))

    def sin_of(k, p):
        return float(np.sin(2.0 * np.pi * (k * p % count) / count))

    def combined(terms):
        value = None
        for factor, term in terms:
            if abs(factor) < 1e-9:
                continue
            if abs(abs(factor) - 1.0) < 1e-9:
                scaled = term
            else:
                scaled = abs(factor) * term
            if value is None:
                value = scaled if factor > 0 else -scaled
            elif factor > 0:
                value = value + scaled
            else:
                value = value - scaled
        return value

    def truncate(field):
        for cut in chunks:
            z = [filtered[field, p, :, cut] for p in range(count)]
            sums = [z[0]] + [z[p] + z[count - p] for p in range(1, half)] + [z[half]]
            gaps = [None] + [z[p] - z[count - p] for p in range(1, half)]
            for k in range(waves):
                cosine = twist_ref[0, k : k + 1, cut]
                sine = twist_ref[1, k : k + 1, cut]
                real = combined([(cos_of(k, p), sums[p]) for p in range(half + 1)])
                imag = combined([(-sin_of(k, p), gaps[p]) for p in range(1, half)])
                if imag is None:
                    turned_re, turned_im = real * cosine, -(real * sine)
                else:
                    turned_re = real * cosine + imag * sine
                    turned_im = imag * cosine - real * sine
                spectrum[k * rows : (k + 1) * rows, cut] = turned_re
                spectrum[block + k * rows : block + (k + 1) * rows, cut] = turned_im
        result = product()
        limit = geo_ref[4]
        for k in range(waves):
            top = slice(k * rows, (k + 1) * rows)
            low = slice(block + k * rows, block + (k + 1) * rows)
            wave = k + count * lane
            wave = jnp.minimum(wave, total - wave).astype(jnp.float32)
            kept = wave <= limit
            spectrum[top, :] = jnp.where(kept, result[top, :lanes] + result[low, lanes:], 0.0)
            spectrum[low, :] = jnp.where(kept, result[low, :lanes] - result[top, lanes:], 0.0)
        result = product()
        scale = 1.0 / total
        for c, cut in enumerate(chunks):
            sin_cut = slice(lanes + 128 * c, lanes + 128 * c + 128)
            reals, imags = [], []
            for k in range(waves):
                top = slice(k * rows, (k + 1) * rows)
                low = slice(block + k * rows, block + (k + 1) * rows)
                factor = scale if k in (0, half) else 2.0 * scale
                cosine = twist_ref[0, k : k + 1, cut] * factor
                sine = twist_ref[1, k : k + 1, cut] * factor
                back_re = result[top, cut] - result[low, sin_cut]
                back_im = result[top, sin_cut] + result[low, cut]
                reals.append(back_re * cosine - back_im * sine)
                imags.append(back_im * cosine + back_re * sine)
            for p in range(half + 1):
                even_part = combined([(cos_of(k, p), reals[k]) for k in range(waves)])
                odd_part = combined([(sin_of(k, p), imags[k]) for k in range(1, half)])
                if odd_part is None:
                    filtered[field, p, :, cut] = even_part
                else:
                    filtered[field, p, :, cut] = even_part - odd_part
                    filtered[field, count - p, :, cut] = even_part + odd_part

    def x_copy(field):
        return pltpu.make_async_copy(x_hbm.at[field], x_ref.at[field], x_sem.at[field])

    table_copies = [
        pltpu.make_async_copy(high_hbm, high_ref, table_sem.at[0]),
        pltpu.make_async_copy(low_hbm, low_ref, table_sem.at[1]),
    ]
    for field in (1, 2, 0, 3, 4):
        x_copy(field).start()
    for copy in table_copies:
        copy.start()

    def turn_rows(field):
        x_copy(field).wait()
        source = jnp.concatenate(
            [x_ref[field], jnp.zeros((lanes - width, x_ref.shape[2]), jnp.float32)], axis=0
        )
        outgoing[field] = source.T

    def send_circles(field):
        over_peers(lambda peer: first_copy(field, peer, me).start())
        own = pl.multiple_of(band * rows, rows)
        states[0, field, me, 8 : 8 + rows, :] = outgoing[field, pl.ds(own, rows), :]

    turn_rows(1)
    expected = count - 1 + crosses_south.astype(jnp.int32) + crosses_north.astype(jnp.int32)
    pl.semaphore_wait(barrier, expected)
    send_circles(1)
    for field in (2, 0):
        turn_rows(field)
        send_circles(field)
    for copy in table_copies:
        copy.wait()

    def advance_field(step_index, carry):
        turn = step_index // fields
        index = lax.rem(step_index, fields)
        field = lax.rem(2 + 3 * index, fields)
        early = turn == 0

        arrivals = jnp.where(early, jnp.where(index == 0, 2, jnp.where(index == 3, 0, 1)), 0)

        def arrival(order, inner_carry):
            arrive(jnp.where(index == 0, 1 + order, field))
            return inner_carry

        lax.fori_loop(0, arrivals, arrival, 0)

        @pl.when(jnp.logical_and(early, index < 2))
        def _():
            turn_rows(3 + index)
            send_circles(3 + index)

        @pl.when(index == 0)
        def _():
            def make_carrier(p):
                wind = wrapped(turn, 1, p)
                carrier[p] = (wind + moved(wind, -1)) * (geo_ref[0] * (1.0 / 120.0))

            over_tiles(make_carrier, 8)

        def along(p):
            value = wrapped(turn, field, p)
            flux = face_flux(
                carrier[p], moved(value, -3), moved(value, -2), moved(value, -1), value,
                moved(value, 1), moved(value, 2),
            )
            zonal = flux - moved(flux, 1)
            filtered[field, p] = jnp.where(inside, zonal, 0.0)

        over_tiles(along, 8)

        @pl.when(field == 1)
        def _():
            def slope(p):
                height = wrapped(turn, 0, p) * wrapped(turn, 3, p)
                drop = (moved(height, 1) - moved(height, -1)) * (0.5 * gravity_scale)
                filtered[field, p] = filtered[field, p] - jnp.where(inside, drop * geo_ref[0], 0.0)

            over_tiles(slope, 8)

        truncate(field)

        lone = jnp.logical_or(early, jnp.logical_or(field == 1, field == 4))
        rims = jnp.where(lone, 1, jnp.where(index == 0, 3, 0))

        def gather_halo(order, inner_carry):
            take_halo(turn, jnp.where(order == 0, field, 3 * (order - 1)))
            return inner_carry

        lax.fori_loop(0, rims, gather_halo, 0)

        @pl.when(index == 0)
        def _():
            def make_crossing(p):
                below = states[turn, 2, p, 7 : 7 + rows, :]
                here = states[turn, 2, p, 8 : 8 + rows, :]
                above = states[turn, 2, p, 9 : 9 + rows, :]
                crossing[0, p] = (below + here) * (geo_ref[1] * (1.0 / 120.0))
                crossing[1, p] = (here + above) * (geo_ref[2] * (1.0 / 120.0))

            over_tiles(make_crossing, 8)

        def across(p):
            around = [
                states[turn, field, p, 8 + offset : 8 + offset + rows, :] for offset in range(-3, 4)
            ]
            lower = face_flux(crossing[0, p], *around[:6])
            upper = face_flux(crossing[1, p], *around[1:])
            change = filtered[field, p] + (lower - upper)
            states[turn + 1, field, p, 8 : 8 + rows, :] = around[3] + time_step * change

        over_tiles(across, 4)

        @pl.when(jnp.logical_or(field == 1, field == 2))
        def _():
            sign = jnp.where(field == 1, time_step, -time_step)

            def turning(p):
                old = states[turn + 1, field, p, 8 : 8 + rows, :]
                wind = states[turn, 3 - field, p, 8 : 8 + rows, :]
                states[turn + 1, field, p, 8 : 8 + rows, :] = old + sign * (geo_ref[3] * wind)

            over_tiles(turning, 8)

        @pl.when(jnp.where(early, 1, 2) == field)
        def _():
            def climb(p):
                old = states[turn + 1, 2, p, 8 : 8 + rows, :]
                upper = states[turn, 0, p, 9 : 9 + rows, :] * states[turn, 3, p, 9 : 9 + rows, :]
                lower = states[turn, 0, p, 7 : 7 + rows, :] * states[turn, 3, p, 7 : 7 + rows, :]
                slope = (upper - lower) * (0.5 * gravity_scale * time_step)
                states[turn + 1, 2, p, 8 : 8 + rows, :] = old - slope

            over_tiles(climb, 8)

        leaving = jnp.where(early, jnp.where(field == 2, 0, jnp.where(field == 1, 2, 1)), 0)

        def spread_halo(order, inner_carry):
            send_halo(1, jnp.where(order == 0, field, 2))
            return inner_carry

        lax.fori_loop(0, leaving, spread_halo, 0)

        @pl.when(turn == 1)
        def _():
            over_peers(lambda peer: last_copy(field, peer, me).start())

        return carry

    lax.fori_loop(0, SUBSTEPS * fields, advance_field, 0)

    own = pl.multiple_of(band * rows, rows)
    for field in (2, 0, 3, 1, 4):
        incoming[field, pl.ds(own, rows), :] = states[2, field, me, 8 : 8 + rows, :]

        def arrived(peer, field=field):
            last_copy(field, peer, peer).wait_recv()

        over_peers(arrived)
        out_ref[field] = incoming[field].T[:width]

    for field in range(fields):

        def sent(peer, field=field):
            first_copy(field, peer, me).wait_send()
            last_copy(field, peer, me).wait_send()

        over_peers(sent)


def circle_advance(state, cutoff_row, lon_count, lat_count):
    fields, _, width, lat_cells = state.shape
    rows = lat_cells // lon_count
    lanes = padded_lanes(width)
    half = lon_count // 2
    me, lat = lax.axis_index("lon"), lax.axis_index("lat")
    band = jnp.where(lat % 2 == 0, me, lon_count - 1 - me)
    centre_cos, centre_sin, face_cos = latitude_rows(
        lat * lat_cells + band * rows, rows, lat_cells * lat_count
    )
    limit = lax.dynamic_slice(cutoff_row, (band * rows,), (rows,))
    table = jnp.stack([
        1.0 / centre_cos, face_cos[:-1] / centre_cos, face_cos[1:] / centre_cos,
        coriolis_scale * centre_sin, limit,
    ])
    geometry = jnp.broadcast_to(table[:, :, None], (5, rows, lanes))
    high, low, twist = circle_tables(lon_count, width, lanes)
    vmem = pl.BlockSpec(memory_space=pltpu.VMEM)
    hbm = pl.BlockSpec(memory_space=pltpu.HBM)
    dma = pltpu.SemaphoreType.DMA
    f32 = jnp.float32
    result = pl.pallas_call(
        functools.partial(circle_kernel, lon_count, width, lat_count),
        out_shape=jax.ShapeDtypeStruct((fields, width, lat_cells), f32),
        in_specs=[hbm, vmem, vmem, hbm, hbm],
        out_specs=vmem,
        scratch_shapes=[
            pltpu.VMEM((fields, width, lat_cells), f32),
            pltpu.VMEM(high.shape, high.dtype),
            pltpu.VMEM(low.shape, low.dtype),
            dma((fields,)), dma((2,)),
            pltpu.VMEM((fields, lat_cells, lanes), f32),
            pltpu.VMEM((3, fields, lon_count, rows + 16, lanes), f32),
            pltpu.VMEM((fields, lat_cells, lanes), f32),
            pltpu.VMEM((fields, lon_count, rows, lanes), f32),
            pltpu.VMEM((lon_count, rows, lanes), f32),
            pltpu.VMEM((2, lon_count, rows, lanes), f32),
            pltpu.VMEM((2 * (half + 1) * rows, lanes), f32),
            pltpu.VMEM((2, 2, fields, 3 * lon_count, lanes), f32),
            pltpu.VMEM((2, 2, fields, 3 * lon_count, lanes), f32),
            dma((fields, lon_count)), dma((fields, lon_count)),
            dma((fields, lon_count)), dma((fields, lon_count)),
            dma((2, 2, fields)), dma((2, 2, fields)),
        ],
        compiler_params=pltpu.CompilerParams(
            collective_id=0, has_side_effects=True, vmem_limit_bytes=62 * 1024 * 1024
        ),
    )(state[:, 0], geometry, twist, high, low)
    return result[:, None]


def padded_lanes(width):
    return -(-(width + 6) // 128) * 128


def fits_circles(state, lon_count, lat_count):
    fields, levels, width, lat_cells = state.shape
    return (
        fields == 5 and levels == 1 and width % 8 == 0 and lat_cells % 128 == 0
        and lon_count % 4 == 0 and lat_cells == 8 * lon_count and lat_count > 1
    )


def shards(state, cutoffs):
    lat_index = lax.axis_index("lat")
    lat_count = lax.axis_size("lat")
    lon_count = lax.axis_size("lon")
    lat_cells = state.shape[3]
    is_south = lat_index == 0
    is_north = lat_index == lat_count - 1
    if fits_circles(state, lon_count, lat_count):
        unfiltered = lon_count * state.shape[2]
        north_row = jnp.where(is_north, jnp.flip(cutoffs[1], 0), unfiltered)
        cutoff_row = jnp.where(is_south, cutoffs[0], north_row).astype(jnp.float32)
        return circle_advance(state, cutoff_row, lon_count, lat_count)
    geometry = latitude_rows(lat_index * lat_cells, lat_cells, lat_cells * lat_count)
    north_row = jnp.where(is_north, jnp.flip(cutoffs[1], 0), -1)
    cutoff_row = jnp.where(is_south, cutoffs[0], north_row).astype(jnp.float32)
    for substep_index in range(SUBSTEPS):
        state = advance(state, geometry, cutoff_row, is_south, is_north)
    return state


def solution(mesh):
    return jax.shard_map(
        shards,
        mesh=mesh,
        in_specs=(P(None, None, "lon", "lat"), P()),
        out_specs=P(None, None, "lon", "lat"),
        check_vma=False,
    )
```

```python
import functools

import jax
import jax.numpy as jnp
import numpy as np
from jax import lax
from jax.experimental import pallas as pl
from jax.experimental.pallas import tpu as pltpu
from jax.sharding import PartitionSpec as P

SUBSTEPS = 2


time_step = 0.5
gravity_scale = 0.25
coriolis_scale = 0.5
wind_sign = (1.0, -1.0, -1.0, 1.0, 1.0)
highest = lax.Precision.HIGHEST
inner_factor = 64
MESH = pl.DeviceIdType.MESH


def passed_along(value, axis, steps):
    count = lax.axis_size(axis)
    pairs = [(source, (source + steps) % count) for source in range(count)]
    return lax.ppermute(value, axis, pairs)


def extended(array, sides, width, wrap):
    for axis, dim in sides:
        peers, length = (lax.axis_size(axis), array.shape[dim])
        up = [(i, (i + 1) % peers) for i in range(peers if wrap else peers - 1)]
        down = [(j, i) for i, j in up]
        last = lax.slice_in_dim(array, length - width, length, axis=dim)
        initial = lax.slice_in_dim(array, 0, width, axis=dim)
        before = lax.ppermute(last, axis, up)
        after = lax.ppermute(initial, axis, down)
        array = jnp.concatenate([before, array, after], axis=dim)
    return array


def interface_flux(halo_padded, transported_field, advection_axis, extent_length):

    def shifted(offset):
        return lax.slice_in_dim(
            halo_padded, offset, offset + extent_length + 1, axis=advection_axis
        )

    far_west, mid_west, near_west, centre, near_east, far_east = [
        shifted(offset) for offset in range(6)
    ]
    interface_velocity = 0.5 * (
        lax.slice_in_dim(transported_field, 2, extent_length + 3, axis=advection_axis)
        + lax.slice_in_dim(transported_field, 3, extent_length + 4, axis=advection_axis)
    )
    central = (
        37.0 * (centre + near_west) - 8.0 * (near_east + mid_west) + (far_east + far_west)
    ) / 60.0
    upwind = (
        far_east - far_west - 5.0 * (near_east - mid_west) + 10.0 * (centre - near_west)
    ) / 60.0
    return interface_velocity * central - jnp.abs(interface_velocity) * upwind


def latitude_rows(first_row, row_count, total_rows):
    centres = (first_row + jnp.arange(row_count, dtype=jnp.int32)).astype(jnp.float32) + 0.5
    centre_cos = jnp.sin(centres * (jnp.pi / total_rows))
    centre_sin = -jnp.cos(centres * (jnp.pi / total_rows))
    faces = first_row + jnp.arange(row_count + 1, dtype=jnp.int32)
    face_cos = jnp.sin(
        jnp.minimum(faces, total_rows - faces).astype(jnp.float32) * (jnp.pi / total_rows)
    )
    return (centre_cos, centre_sin, face_cos)


def geopotential(fields):
    layer_mass = fields[0] * fields[3]
    return gravity_scale * jnp.flip(jnp.cumsum(jnp.flip(layer_mass, 0), axis=0), 0)


def zonal_tendency(lon_padded, centre_cos):
    lon_cells = lon_padded.shape[2] - 6
    face_fluxes = interface_flux(lon_padded, lon_padded[1:2], 2, lon_cells)
    zonal = face_fluxes[:, :, :-1] - face_fluxes[:, :, 1:]
    height = geopotential(lon_padded)
    height_slope = 0.5 * (height[:, 4 : lon_cells + 4] - height[:, 2 : lon_cells + 2])
    zonal = jnp.concatenate([zonal[:1], zonal[1:2] - height_slope[None], zonal[2:]], axis=0)
    return zonal / centre_cos


def phase_table(first, second, modulus, total):
    angle = (first[:, None] * second[None, :] % modulus).astype(jnp.float32) * (
        2.0 * jnp.pi / total
    )
    return (jnp.cos(angle), jnp.sin(angle))


def truncate_rows(rows, row_limit, lon_total):
    row_count = rows.shape[0]
    outer = lon_total // inner_factor
    outer_index = jnp.arange(outer, dtype=jnp.int32)
    inner_index = jnp.arange(inner_factor, dtype=jnp.int32)
    outer_cos, outer_sin = phase_table(outer_index, outer_index, outer, outer)
    twist_cos, twist_sin = phase_table(outer_index, inner_index, lon_total, lon_total)
    inner_cos, inner_sin = phase_table(inner_index, inner_index, inner_factor, inner_factor)
    folded = rows.reshape(row_count, outer, inner_factor)
    first_re = jnp.einsum("rpq,pk->rkq", folded, outer_cos, precision=highest)
    first_im = -jnp.einsum("rpq,pk->rkq", folded, outer_sin, precision=highest)
    turned_re = first_re * twist_cos + first_im * twist_sin
    turned_im = first_im * twist_cos - first_re * twist_sin
    spec_re = jnp.einsum("rkq,qj->rkj", turned_re, inner_cos, precision=highest) + jnp.einsum(
        "rkq,qj->rkj", turned_im, inner_sin, precision=highest
    )
    spec_im = jnp.einsum("rkq,qj->rkj", turned_im, inner_cos, precision=highest) - jnp.einsum(
        "rkq,qj->rkj", turned_re, inner_sin, precision=highest
    )
    wave = outer_index[:, None] + outer * inner_index[None, :]
    wave = jnp.minimum(wave, lon_total - wave).astype(jnp.float32)
    kept = wave[None, :, :] <= row_limit[:, None, None]
    spec_re = jnp.where(kept, spec_re, 0.0)
    spec_im = jnp.where(kept, spec_im, 0.0)
    back_re = jnp.einsum("rkj,qj->rkq", spec_re, inner_cos, precision=highest) - jnp.einsum(
        "rkj,qj->rkq", spec_im, inner_sin, precision=highest
    )
    back_im = jnp.einsum("rkj,qj->rkq", spec_re, inner_sin, precision=highest) + jnp.einsum(
        "rkj,qj->rkq", spec_im, inner_cos, precision=highest
    )
    untwist_re = back_re * twist_cos - back_im * twist_sin
    untwist_im = back_re * twist_sin + back_im * twist_cos
    result = jnp.einsum("rkq,pk->rpq", untwist_re, outer_cos, precision=highest) - jnp.einsum(
        "rkq,pk->rpq", untwist_im, outer_sin, precision=highest
    )
    return result.reshape(row_count, lon_total) / lon_total


def crossing_rims(state, is_south, is_north):
    lat_cells = state.shape[3]
    lon_count = lax.axis_size("lon")
    wind_flip = jnp.array(wind_sign, dtype=jnp.float32)[:, None, None, None]
    pole_rows = jnp.where(is_south, state[..., 0:2], state[..., lat_cells - 2 :])
    partner = passed_along(pole_rows, "lon", lon_count // 2) * wind_flip
    lat_halo = extended(state, (("lat", 3),), 3, False)
    south_rim = jnp.where(
        is_south,
        jnp.concatenate([lat_halo[..., 0:1], partner[..., 1:2], partner[..., 0:1]], axis=3),
        lat_halo[..., 0:3],
    )
    north_rim = jnp.where(
        is_north,
        jnp.concatenate(
            [partner[..., 1:2], partner[..., 0:1], lat_halo[..., lat_cells + 5 :]], axis=3
        ),
        lat_halo[..., lat_cells + 3 :],
    )
    return jnp.concatenate([south_rim, state, north_rim], axis=3)


def advance(state, geometry, cutoff_row, is_south, is_north):
    centre_cos, centre_sin, face_cos = geometry
    field_count, level_count, lon_cells, lat_cells = state.shape
    lon_count = lax.axis_size("lon")
    lon_total = lon_cells * lon_count
    lon_padded = extended(state, (("lon", 2),), 3, True)
    zonal = zonal_tendency(lon_padded, centre_cos)
    row_block = jnp.transpose(zonal, (0, 1, 3, 2)).reshape(lon_count, -1, lon_cells)
    row_limits = jnp.broadcast_to(cutoff_row, (field_count, level_count, lat_cells)).reshape(
        lon_count, -1, 1
    )
    values = lax.all_to_all(row_block, "lon", split_axis=0, concat_axis=2, tiled=True)
    limits = lax.all_to_all(row_limits, "lon", split_axis=0, concat_axis=2, tiled=True)
    spread = truncate_rows(values[0], limits[0, :, 0], lon_total)[None]
    returned = lax.all_to_all(spread, "lon", split_axis=2, concat_axis=0, tiled=True)
    filtered = jnp.transpose(
        returned.reshape(field_count, level_count, lat_cells, lon_cells), (0, 1, 3, 2)
    )
    zonal = jnp.where(jnp.logical_or(is_south, is_north), filtered, zonal)
    lat_padded = crossing_rims(state, is_south, is_north)
    merid_fluxes = interface_flux(lat_padded, lat_padded[2:3], 3, lat_cells) * face_cos
    meridional = (merid_fluxes[..., :-1] - merid_fluxes[..., 1:]) / centre_cos
    height = geopotential(lat_padded)
    north_slope = 0.5 * (height[..., 4 : lat_cells + 4] - height[..., 2 : lat_cells + 2])
    turning = coriolis_scale * centre_sin
    flux_tendency = zonal + meridional
    east_wind = flux_tendency[1] + turning * state[2]
    north_wind = flux_tendency[2] - turning * state[1] - north_slope
    flux_tendency = jnp.concatenate(
        [flux_tendency[:1], east_wind[None], north_wind[None], flux_tendency[3:]], axis=0
    )
    return state + time_step * flux_tendency


def circle_tables(count, width, lanes):
    total = count * width
    inner = np.arange(width)
    angle = 2.0 * np.pi * (inner[:, None] * inner[None, :] % width) / width
    table = np.zeros((lanes, 2 * lanes), np.float32)
    table[:width, :width] = np.cos(angle)
    table[:width, lanes : lanes + width] = np.sin(angle)
    high = table.astype(jnp.bfloat16)
    low = (table - high.astype(np.float32)).astype(jnp.bfloat16)
    outer = np.arange(count // 2 + 1)
    turn = 2.0 * np.pi * (outer[:, None] * np.arange(lanes)[None, :] % total) / total
    twist = np.stack([np.cos(turn), np.sin(turn)]).astype(np.float32)
    return high, low, twist


def circle_kernel(
    count, width, bands, x_hbm, geo_ref, twist_ref, high_hbm, low_hbm, out_ref,
    x_ref, high_ref, low_ref, x_sem, table_sem, outgoing, states, incoming, filtered, carrier, crossing, spectrum, halo_out, halo_in,
    first_send, first_recv, last_send, last_recv, halo_send, halo_recv,
):
    fields = x_ref.shape[0]
    lanes = outgoing.shape[2]
    rows = geo_ref.shape[1]
    half = count // 2
    total = count * width
    me = lax.axis_index("lon")
    lat = lax.axis_index("lat")
    even = lax.rem(lat, 2) == 0

    def band_of(device):
        return jnp.where(even, device, count - 1 - device)

    band = band_of(me)
    at_south = jnp.logical_and(band == 0, lat == 0)
    at_north = jnp.logical_and(band == count - 1, lat == bands - 1)
    step = jnp.where(even, 1, -1)
    south_lon = jnp.where(band == 0, me, me - step)
    south_lat = jnp.where(band == 0, lat - 1, lat)
    north_lon = jnp.where(band == count - 1, me, me + step)
    north_lat = jnp.where(band == count - 1, lat + 1, lat)
    lane = lax.broadcasted_iota(jnp.int32, (rows, lanes), 1)
    inside = lane < width

    barrier = pltpu.get_barrier_semaphore()

    def greet(offset, carry):
        peer = lax.rem(me + offset, count)
        pl.semaphore_signal(barrier, inc=1, device_id={"lon": peer, "lat": lat}, device_id_type=MESH)
        return carry

    lax.fori_loop(1, count, greet, 0)
    crosses_south = jnp.logical_and(band == 0, lat > 0)
    crosses_north = jnp.logical_and(band == count - 1, lat < bands - 1)

    @pl.when(crosses_south)
    def _():
        pl.semaphore_signal(barrier, inc=1, device_id={"lon": me, "lat": lat - 1}, device_id_type=MESH)

    @pl.when(crosses_north)
    def _():
        pl.semaphore_signal(barrier, inc=1, device_id={"lon": me, "lat": lat + 1}, device_id_type=MESH)

    def first_copy(field, peer, slot):
        start = pl.multiple_of(band_of(peer) * rows, rows)
        return pltpu.make_async_remote_copy(
            src_ref=outgoing.at[field, pl.ds(start, rows), :],
            dst_ref=states.at[0, field, slot, pl.ds(8, rows), :],
            send_sem=first_send.at[field, peer],
            recv_sem=first_recv.at[field, slot],
            device_id={"lon": peer, "lat": lat},
            device_id_type=MESH,
        )

    def last_copy(field, peer, owner):
        start = pl.multiple_of(band_of(owner) * rows, rows)
        return pltpu.make_async_remote_copy(
            src_ref=states.at[2, field, peer, pl.ds(8, rows), :],
            dst_ref=incoming.at[field, pl.ds(start, rows), :],
            send_sem=last_send.at[field, peer],
            recv_sem=last_recv.at[field, owner],
            device_id={"lon": peer, "lat": lat},
            device_id_type=MESH,
        )

    def over_peers(action):
        def one(offset, carry):
            action(lax.rem(me + offset, count))
            return carry

        lax.fori_loop(1, count, one, 0)

    def halo_copy(turn, side, field):
        return pltpu.make_async_remote_copy(
            src_ref=halo_out.at[turn, side, field],
            dst_ref=halo_in.at[turn, 1 - side, field],
            send_sem=halo_send.at[turn, side, field],
            recv_sem=halo_recv.at[turn, 1 - side, field],
            device_id={
                "lon": south_lon if side == 0 else north_lon,
                "lat": south_lat if side == 0 else north_lat,
            },
            device_id_type=MESH,
        )

    def send_halo(turn, field):
        for p in range(count):
            halo_out[turn, 0, field, 3 * p : 3 * p + 3, :] = states[turn, field, p, 8:11, :]
            halo_out[turn, 1, field, 3 * p : 3 * p + 3, :] = states[turn, field, p, rows + 5 : rows + 8, :]

        @pl.when(jnp.logical_not(at_south))
        def _():
            halo_copy(turn, 0, field).start()

        @pl.when(jnp.logical_not(at_north))
        def _():
            halo_copy(turn, 1, field).start()

    def take_halo(turn, field):
        sign = jnp.where(jnp.logical_or(field == 1, field == 2), -1.0, 1.0)

        @pl.when(jnp.logical_not(at_south))
        def _():
            copy = halo_copy(turn, 0, field)
            copy.wait_send()
            arrival = pltpu.make_async_remote_copy(
                src_ref=halo_out.at[turn, 0, field],
                dst_ref=halo_in.at[turn, 0, field],
                send_sem=halo_send.at[turn, 0, field],
                recv_sem=halo_recv.at[turn, 0, field],
                device_id={"lon": south_lon, "lat": south_lat},
                device_id_type=MESH,
            )
            arrival.wait_recv()
            for p in range(count):
                states[turn, field, p, 5:8, :] = halo_in[turn, 0, field, 3 * p : 3 * p + 3, :]

        @pl.when(at_south)
        def _():
            for p in range(count):
                for m in range(3):
                    states[turn, field, p, 7 - m : 8 - m, :] = (
                        sign * states[turn, field, (p + half) % count, 8 + m : 9 + m, :]
                    )

        @pl.when(jnp.logical_not(at_north))
        def _():
            copy = halo_copy(turn, 1, field)
            copy.wait_send()
            arrival = pltpu.make_async_remote_copy(
                src_ref=halo_out.at[turn, 1, field],
                dst_ref=halo_in.at[turn, 1, field],
                send_sem=halo_send.at[turn, 1, field],
                recv_sem=halo_recv.at[turn, 1, field],
                device_id={"lon": north_lon, "lat": north_lat},
                device_id_type=MESH,
            )
            arrival.wait_recv()
            for p in range(count):
                states[turn, field, p, rows + 8 : rows + 11, :] = halo_in[
                    turn, 1, field, 3 * p : 3 * p + 3, :
                ]

        @pl.when(at_north)
        def _():
            for p in range(count):
                for m in range(3):
                    states[turn, field, p, rows + 8 + m : rows + 9 + m, :] = (
                        sign
                        * states[turn, field, (p + half) % count, rows + 7 - m : rows + 8 - m, :]
                    )

    def arrive(field):
        def one(peer):
            first_copy(field, peer, peer).wait_recv()

        over_peers(one)
        send_halo(0, field)

    def wrapped(turn, field, p):
        east = lax.rem(p + 1, count)
        west = lax.rem(p + count - 1, count)
        core = states[turn, field, p, 8 : 8 + rows, :]
        after = pltpu.roll(states[turn, field, east, 8 : 8 + rows, :], width, 1)
        before = pltpu.roll(states[turn, field, west, 8 : 8 + rows, :], lanes - width, 1)
        middle = width + (lanes - width) // 2
        return jnp.where(inside, core, jnp.where(lane < middle, after, before))

    def moved(value, offset):
        return pltpu.roll(value, (-offset) % lanes, 1)

    def face_flux(carrying, m3, m2, m1, c0, p1, p2):
        central = 37.0 * (c0 + m1) - 8.0 * (p1 + m2) + (p2 + m3)
        upwind = (p2 - m3) - 5.0 * (p1 - m2) + 10.0 * (c0 - m1)
        return carrying * central - jnp.abs(carrying) * upwind

    def over_tiles(action, group=2):
        def one(block, carry):
            for inner in range(group):
                action(block * group + inner)
            return carry

        lax.fori_loop(0, count // group, one, 0)

    chunks = [slice(128 * c, 128 * c + 128) for c in range(lanes // 128)]
    waves = half + 1
    block = waves * rows

    def product():
        value = spectrum[...]
        high = value.astype(jnp.bfloat16)
        low = (value - high.astype(jnp.float32)).astype(jnp.bfloat16)
        weights = high_ref[...]
        both = jnp.dot(
            jnp.concatenate([high, low], axis=0), weights, preferred_element_type=jnp.float32
        )
        rest = jnp.dot(high, low_ref[...], preferred_element_type=jnp.float32)
        return both[: 2 * block] + both[2 * block :] + rest

    def cos_of(k, p):
        return float(np.cos(2.0 * np.pi * (k * p % count) / count))

    def sin_of(k, p):
        return float(np.sin(2.0 * np.pi * (k * p % count) / count))

    def combined(terms):
        value = None
        for factor, term in terms:
            if abs(factor) < 1e-9:
                continue
            if abs(abs(factor) - 1.0) < 1e-9:
                scaled = term
            else:
                scaled = abs(factor) * term
            if value is None:
                value = scaled if factor > 0 else -scaled
            elif factor > 0:
                value = value + scaled
            else:
                value = value - scaled
        return value

    def truncate(field):
        for cut in chunks:
            z = [filtered[field, p, :, cut] for p in range(count)]
            sums = [z[0]] + [z[p] + z[count - p] for p in range(1, half)] + [z[half]]
            gaps = [None] + [z[p] - z[count - p] for p in range(1, half)]
            for k in range(waves):
                cosine = twist_ref[0, k : k + 1, cut]
                sine = twist_ref[1, k : k + 1, cut]
                real = combined([(cos_of(k, p), sums[p]) for p in range(half + 1)])
                imag = combined([(-sin_of(k, p), gaps[p]) for p in range(1, half)])
                if imag is None:
                    turned_re, turned_im = real * cosine, -(real * sine)
                else:
                    turned_re = real * cosine + imag * sine
                    turned_im = imag * cosine - real * sine
                spectrum[k * rows : (k + 1) * rows, cut] = turned_re
                spectrum[block + k * rows : block + (k + 1) * rows, cut] = turned_im
        result = product()
        limit = geo_ref[4]
        for k in range(waves):
            top = slice(k * rows, (k + 1) * rows)
            low = slice(block + k * rows, block + (k + 1) * rows)
            wave = k + count * lane
            wave = jnp.minimum(wave, total - wave).astype(jnp.float32)
            kept = wave <= limit
            spectrum[top, :] = jnp.where(kept, result[top, :lanes] + result[low, lanes:], 0.0)
            spectrum[low, :] = jnp.where(kept, result[low, :lanes] - result[top, lanes:], 0.0)
        result = product()
        scale = 1.0 / total
        for c, cut in enumerate(chunks):
            sin_cut = slice(lanes + 128 * c, lanes + 128 * c + 128)
            reals, imags = [], []
            for k in range(waves):
                top = slice(k * rows, (k + 1) * rows)
                low = slice(block + k * rows, block + (k + 1) * rows)
                factor = scale if k in (0, half) else 2.0 * scale
                cosine = twist_ref[0, k : k + 1, cut] * factor
                sine = twist_ref[1, k : k + 1, cut] * factor
                back_re = result[top, cut] - result[low, sin_cut]
                back_im = result[top, sin_cut] + result[low, cut]
                reals.append(back_re * cosine - back_im * sine)
                imags.append(back_im * cosine + back_re * sine)
            for p in range(half + 1):
                even_part = combined([(cos_of(k, p), reals[k]) for k in range(waves)])
                odd_part = combined([(sin_of(k, p), imags[k]) for k in range(1, half)])
                if odd_part is None:
                    filtered[field, p, :, cut] = even_part
                else:
                    filtered[field, p, :, cut] = even_part - odd_part
                    filtered[field, count - p, :, cut] = even_part + odd_part

    def x_copy(field):
        return pltpu.make_async_copy(x_hbm.at[field], x_ref.at[field], x_sem.at[field])

    table_copies = [
        pltpu.make_async_copy(high_hbm, high_ref, table_sem.at[0]),
        pltpu.make_async_copy(low_hbm, low_ref, table_sem.at[1]),
    ]
    for field in (1, 2, 0, 3, 4):
        x_copy(field).start()
    for copy in table_copies:
        copy.start()

    def turn_rows(field):
        x_copy(field).wait()
        source = jnp.concatenate(
            [x_ref[field], jnp.zeros((lanes - width, x_ref.shape[2]), jnp.float32)], axis=0
        )
        outgoing[field] = source.T

    def send_circles(field):
        over_peers(lambda peer: first_copy(field, peer, me).start())
        own = pl.multiple_of(band * rows, rows)
        states[0, field, me, 8 : 8 + rows, :] = outgoing[field, pl.ds(own, rows), :]

    turn_rows(1)
    expected = count - 1 + crosses_south.astype(jnp.int32) + crosses_north.astype(jnp.int32)
    pl.semaphore_wait(barrier, expected)
    send_circles(1)
    for field in (2,):
        turn_rows(field)
        send_circles(field)
    for copy in table_copies:
        copy.wait()

    def advance_field(step_index, carry):
        turn = step_index // fields
        index = lax.rem(step_index, fields)
        field = lax.rem(2 + 3 * index, fields)
        early = turn == 0

        arrivals = jnp.where(early, jnp.where(index == 0, 2, jnp.where(index == 3, 0, 1)), 0)

        def arrival(order, inner_carry):
            coming = jnp.where(index == 0, 1 + order, field)
            arrive(coming)

            @pl.when(coming < 3)
            def _():
                ahead = jnp.where(coming == 1, 0, jnp.where(coming == 2, 3, 4))
                turn_rows(ahead)
                send_circles(ahead)

            return inner_carry

        lax.fori_loop(0, arrivals, arrival, 0)

        @pl.when(step_index < 0)
        def _():
            turn_rows(3 + index)
            send_circles(3 + index)

        @pl.when(index == 0)
        def _():
            def make_carrier(p):
                wind = wrapped(turn, 1, p)
                carrier[p] = (wind + moved(wind, -1)) * (geo_ref[0] * (1.0 / 120.0))

            over_tiles(make_carrier, 8)

        def along(p):
            value = wrapped(turn, field, p)
            flux = face_flux(
                carrier[p], moved(value, -3), moved(value, -2), moved(value, -1), value,
                moved(value, 1), moved(value, 2),
            )
            zonal = flux - moved(flux, 1)
            filtered[field, p] = jnp.where(inside, zonal, 0.0)

        over_tiles(along, 8)

        @pl.when(field == 1)
        def _():
            def slope(p):
                height = wrapped(turn, 0, p) * wrapped(turn, 3, p)
                drop = (moved(height, 1) - moved(height, -1)) * (0.5 * gravity_scale)
                filtered[field, p] = filtered[field, p] - jnp.where(inside, drop * geo_ref[0], 0.0)

            over_tiles(slope, 8)

        truncate(field)

        lone = jnp.logical_or(early, jnp.logical_or(field == 1, field == 4))
        rims = jnp.where(lone, 1, jnp.where(index == 0, 3, 0))

        def gather_halo(order, inner_carry):
            take_halo(turn, jnp.where(order == 0, field, 3 * (order - 1)))
            return inner_carry

        lax.fori_loop(0, rims, gather_halo, 0)

        @pl.when(index == 0)
        def _():
            def make_crossing(p):
                below = states[turn, 2, p, 7 : 7 + rows, :]
                here = states[turn, 2, p, 8 : 8 + rows, :]
                above = states[turn, 2, p, 9 : 9 + rows, :]
                crossing[0, p] = (below + here) * (geo_ref[1] * (1.0 / 120.0))
                crossing[1, p] = (here + above) * (geo_ref[2] * (1.0 / 120.0))

            over_tiles(make_crossing, 8)

        def across(p):
            around = [
                states[turn, field, p, 8 + offset : 8 + offset + rows, :] for offset in range(-3, 4)
            ]
            lower = face_flux(crossing[0, p], *around[:6])
            upper = face_flux(crossing[1, p], *around[1:])
            change = filtered[field, p] + (lower - upper)
            states[turn + 1, field, p, 8 : 8 + rows, :] = around[3] + time_step * change

        over_tiles(across, 4)

        @pl.when(jnp.logical_or(field == 1, field == 2))
        def _():
            sign = jnp.where(field == 1, time_step, -time_step)

            def turning(p):
                old = states[turn + 1, field, p, 8 : 8 + rows, :]
                wind = states[turn, 3 - field, p, 8 : 8 + rows, :]
                states[turn + 1, field, p, 8 : 8 + rows, :] = old + sign * (geo_ref[3] * wind)

            over_tiles(turning, 8)

        @pl.when(jnp.where(early, 1, 2) == field)
        def _():
            def climb(p):
                old = states[turn + 1, 2, p, 8 : 8 + rows, :]
                upper = states[turn, 0, p, 9 : 9 + rows, :] * states[turn, 3, p, 9 : 9 + rows, :]
                lower = states[turn, 0, p, 7 : 7 + rows, :] * states[turn, 3, p, 7 : 7 + rows, :]
                slope = (upper - lower) * (0.5 * gravity_scale * time_step)
                states[turn + 1, 2, p, 8 : 8 + rows, :] = old - slope

            over_tiles(climb, 8)

        leaving = jnp.where(early, jnp.where(field == 2, 0, jnp.where(field == 1, 2, 1)), 0)

        def spread_halo(order, inner_carry):
            send_halo(1, jnp.where(order == 0, field, 2))
            return inner_carry

        lax.fori_loop(0, leaving, spread_halo, 0)

        @pl.when(turn == 1)
        def _():
            over_peers(lambda peer: last_copy(field, peer, me).start())

        return carry

    lax.fori_loop(0, SUBSTEPS * fields, advance_field, 0)

    own = pl.multiple_of(band * rows, rows)
    for field in (2, 0, 3, 1, 4):
        incoming[field, pl.ds(own, rows), :] = states[2, field, me, 8 : 8 + rows, :]

        def arrived(peer, field=field):
            last_copy(field, peer, peer).wait_recv()

        over_peers(arrived)
        out_ref[field] = incoming[field].T[:width]

    for field in range(fields):

        def sent(peer, field=field):
            first_copy(field, peer, me).wait_send()
            last_copy(field, peer, me).wait_send()

        over_peers(sent)


def circle_advance(state, cutoff_row, lon_count, lat_count):
    fields, _, width, lat_cells = state.shape
    rows = lat_cells // lon_count
    lanes = padded_lanes(width)
    half = lon_count // 2
    me, lat = lax.axis_index("lon"), lax.axis_index("lat")
    band = jnp.where(lat % 2 == 0, me, lon_count - 1 - me)
    centre_cos, centre_sin, face_cos = latitude_rows(
        lat * lat_cells + band * rows, rows, lat_cells * lat_count
    )
    limit = lax.dynamic_slice(cutoff_row, (band * rows,), (rows,))
    table = jnp.stack([
        1.0 / centre_cos, face_cos[:-1] / centre_cos, face_cos[1:] / centre_cos,
        coriolis_scale * centre_sin, limit,
    ])
    geometry = jnp.broadcast_to(table[:, :, None], (5, rows, lanes))
    high, low, twist = circle_tables(lon_count, width, lanes)
    vmem = pl.BlockSpec(memory_space=pltpu.VMEM)
    hbm = pl.BlockSpec(memory_space=pltpu.HBM)
    dma = pltpu.SemaphoreType.DMA
    f32 = jnp.float32
    keep = lambda value: pltpu.with_memory_space_constraint(value, pltpu.HBM)
    result = pl.pallas_call(
        functools.partial(circle_kernel, lon_count, width, lat_count),
        out_shape=jax.ShapeDtypeStruct((fields, width, lat_cells), f32),
        in_specs=[hbm, vmem, vmem, hbm, hbm],
        out_specs=vmem,
        scratch_shapes=[
            pltpu.VMEM((fields, width, lat_cells), f32),
            pltpu.VMEM(high.shape, high.dtype),
            pltpu.VMEM(low.shape, low.dtype),
            dma((fields,)), dma((2,)),
            pltpu.VMEM((fields, lat_cells, lanes), f32),
            pltpu.VMEM((3, fields, lon_count, rows + 16, lanes), f32),
            pltpu.VMEM((fields, lat_cells, lanes), f32),
            pltpu.VMEM((fields, lon_count, rows, lanes), f32),
            pltpu.VMEM((lon_count, rows, lanes), f32),
            pltpu.VMEM((2, lon_count, rows, lanes), f32),
            pltpu.VMEM((2 * (half + 1) * rows, lanes), f32),
            pltpu.VMEM((2, 2, fields, 3 * lon_count, lanes), f32),
            pltpu.VMEM((2, 2, fields, 3 * lon_count, lanes), f32),
            dma((fields, lon_count)), dma((fields, lon_count)),
            dma((fields, lon_count)), dma((fields, lon_count)),
            dma((2, 2, fields)), dma((2, 2, fields)),
        ],
        compiler_params=pltpu.CompilerParams(
            collective_id=0, has_side_effects=True, vmem_limit_bytes=48 * 1024 * 1024
        ),
    )(keep(state[:, 0]), geometry, twist, keep(jnp.asarray(high)), keep(jnp.asarray(low)))
    return result[:, None]


def padded_lanes(width):
    return -(-(width + 6) // 128) * 128


def fits_circles(state, lon_count, lat_count):
    fields, levels, width, lat_cells = state.shape
    return (
        fields == 5 and levels == 1 and width % 8 == 0 and lat_cells % 128 == 0
        and lon_count % 4 == 0 and lat_cells == 8 * lon_count and lat_count > 1
    )


def shards(state, cutoffs):
    lat_index = lax.axis_index("lat")
    lat_count = lax.axis_size("lat")
    lon_count = lax.axis_size("lon")
    lat_cells = state.shape[3]
    is_south = lat_index == 0
    is_north = lat_index == lat_count - 1
    if fits_circles(state, lon_count, lat_count):
        unfiltered = lon_count * state.shape[2]
        north_row = jnp.where(is_north, jnp.flip(cutoffs[1], 0), unfiltered)
        cutoff_row = jnp.where(is_south, cutoffs[0], north_row).astype(jnp.float32)
        return circle_advance(state, cutoff_row, lon_count, lat_count)
    geometry = latitude_rows(lat_index * lat_cells, lat_cells, lat_cells * lat_count)
    north_row = jnp.where(is_north, jnp.flip(cutoffs[1], 0), -1)
    cutoff_row = jnp.where(is_south, cutoffs[0], north_row).astype(jnp.float32)
    for substep_index in range(SUBSTEPS):
        state = advance(state, geometry, cutoff_row, is_south, is_north)
    return state


def solution(mesh):
    return jax.shard_map(
        shards,
        mesh=mesh,
        in_specs=(P(None, None, "lon", "lat"), P()),
        out_specs=P(None, None, "lon", "lat"),
        check_vma=False,
    )
```
